256 devices in a mesh: cell: 32 (over y, x, core), lane: 8 (over z).
Axes of the slice: x: 4, y: 4, z: 8, core: 2. Of those that a mesh axis runs over, the one named last changes fastest.
Arguments:
- channel: float32 [32, 64, 2, 16, 256], P('cell', 'lane'), may hold values from -8 to 8
- symbols: bfloat16 [32, 16, 2, 2, 3072], P('cell'), may hold values from -4 to 4
- layers: int32 [32, 256], P('cell'), may hold values from 0 to 16, as said below
- user_ids: int32 [32, 16, 256], P('cell'), may hold values from 0 to 127
- user_power: float32 [32, 128], P('cell'), may hold values from 0.25 to 4
- neighbours: int32 [32, 6], replicated, may hold values from 0 to 31, as said below
- coupling: float32 [32, 6], replicated, may hold values from 0.05 to 0.5
Outputs:
- time_samples: float32 [32, 64, 2, 2, 4096], P('cell', 'lane')
The draws below stay inside these ranges and needn't reach their ends.
Inputs may be any that keep to these rules, and one draw needn't show every extreme that they name: Some block of some cell has all 16 layers granted; for every index of the cell axis and every group of 8 aligned blocks, the layers of that index's 1 cells over the group sum to at most 48, and to exactly 48 for some index and group. `neighbours`: a cell never lists itself.
All inputs are finite; a program needn't handle non-finite values.
Results may differ from the reference program's by a relative error of at most 0.0029.
Values may be sent and summed in bfloat16 or wider, within the bound.
A program may use at most 64 MiB of HBM per device.

```python
import math
import jax
import jax.numpy as jnp
from jax import lax

TX_ANTENNA_COUNT = 64
MAX_LAYERS = 16
PRBS = 256
SUBC = 12
NFFT = 4096
SYMS = 2
USERS = 128
NEIGH = 6
NS_STEPS = 6
CELL_DEV = 1
POOL_CELL_COUNT = 32
SUBCARRIERS = 3072
BLOCK_GROUP = 8
PACK_CAP = 48


def draw_channel(key, part):
    base_station_key, row_key_split, antenna_key = jax.random.split(key, 3)
    shape = (POOL_CELL_COUNT, TX_ANTENNA_COUNT, 2, MAX_LAYERS, PRBS)
    base = jax.random.normal(base_station_key, shape, jnp.float32)
    row_scale = jnp.exp(jax.random.uniform(row_key_split, (POOL_CELL_COUNT, 1, 1, MAX_LAYERS, PRBS), jnp.float32, math.log(0.3), math.log(3.0)))
    antenna_gain_scale = jnp.exp(jax.random.uniform(antenna_key, (POOL_CELL_COUNT, TX_ANTENNA_COUNT, 1, 1, 1), jnp.float32, math.log(0.3), math.log(3.0)))
    values = base * row_scale * antenna_gain_scale * (0.5 / math.sqrt(TX_ANTENNA_COUNT))
    return jnp.clip(values, -8.0, 8.0).astype(jnp.float32)


def draw_layers(key, part):
    key_level, base_station_key, key_dev, key_group = jax.random.split(key, 4)
    level = jax.random.randint(key_level, (POOL_CELL_COUNT, 1), 2, MAX_LAYERS + 1)
    base = jax.random.randint(base_station_key, (POOL_CELL_COUNT, PRBS), 0, level + 1)
    groups = POOL_CELL_COUNT // CELL_DEV
    grouped = base.reshape(groups, CELL_DEV, groups, BLOCK_GROUP)
    totals = jnp.sum(grouped, axis=(1, 3), keepdims=True)
    capped = jnp.where(totals > PACK_CAP, grouped * PACK_CAP // jnp.maximum(totals, 1), grouped)
    entries = CELL_DEV * BLOCK_GROUP
    flat_pos = lax.broadcasted_iota(jnp.int32, (1, CELL_DEV, 1, BLOCK_GROUP), 1) * BLOCK_GROUP + lax.broadcasted_iota(jnp.int32, (1, CELL_DEV, 1, BLOCK_GROUP), 3)
    leftover = PACK_CAP - MAX_LAYERS
    spread_over = max(entries - 1, 1)
    share = leftover // spread_over
    extra = leftover % spread_over
    filled = jnp.where(flat_pos == 0, MAX_LAYERS, share + (flat_pos - 1 < extra).astype(jnp.int32))
    pick_dev = jax.random.randint(key_dev, (), 0, groups)
    pick_group = jax.random.randint(key_group, (), 0, groups)
    dev_iota = lax.broadcasted_iota(jnp.int32, (groups, 1, groups, 1), 0)
    group_iota = lax.broadcasted_iota(jnp.int32, (groups, 1, groups, 1), 2)
    chosen = jnp.logical_and(dev_iota == pick_dev, group_iota == pick_group)
    result = jnp.where(chosen, filled, capped)
    return result.reshape(POOL_CELL_COUNT, PRBS).astype(jnp.int32)


def draw_neighbours(key, part):
    offsets = jax.random.randint(key, (POOL_CELL_COUNT, NEIGH), 1, POOL_CELL_COUNT)
    rows = jnp.arange(POOL_CELL_COUNT, dtype=jnp.int32)[:, None]
    return ((rows + offsets) % POOL_CELL_COUNT).astype(jnp.int32)


def touch_ends(values, rng, smallest, high):
    longest = values.shape.index(max(values.shape))
    spots = []
    for shift in (0, 1):
        where = [jax.random.randint(jax.random.fold_in(rng, axis), (), 0, length) for axis, length in enumerate(values.shape)]
        where[longest] = (where[longest] + shift) % values.shape[longest]
        spots.append(tuple(where))
    return values.at[spots[0]].set(smallest).at[spots[1]].set(high)


def steps_of(own_key, shape, pieces, low, largest):
    factor_of = 1.0
    for position, parts in pieces:
        draws = jax.random.uniform(jax.random.fold_in(jax.random.fold_in(own_key, 6), position), (parts,), jnp.float32, low / len(pieces), largest / len(pieces))
        factor_of = factor_of * jnp.repeat(jnp.exp(draws), shape[position] // parts).reshape((-1,) + (1,) * (len(shape) - 1 - position))
    return factor_of


def normal_values(rng, shape, scale, reach, cuts=(), held_as=jnp.bfloat16):
    values = jax.random.normal(rng, shape, jnp.float32) * scale
    if len(cuts) > 0:
        values = steps_of(rng, shape, cuts, -0.22, 0.18) * values
    return jnp.clip(values, min=-reach, max=reach).astype(held_as)


def setup_inputs(seed: int = 0) -> dict:
    splits = jax.random.split(jax.random.key(seed), 8)
    channel = draw_channel(jax.random.fold_in(splits[7], 71), 0)
    symbols = normal_values(splits[1], (POOL_CELL_COUNT, MAX_LAYERS, 2, SYMS, SUBCARRIERS), 0.7, 4.0, ((0, 32),))
    layers = draw_layers(jax.random.fold_in(splits[7], 71), 0)
    user_ids = touch_ends(jax.random.randint(splits[3], (POOL_CELL_COUNT, MAX_LAYERS, PRBS), 0, USERS), jax.random.fold_in(splits[3], 1), 0, USERS - 1).astype(jnp.int32)
    user_power = jnp.clip(jnp.exp(math.log(4.0) - 2.7725887 * jax.random.uniform(splits[4], (POOL_CELL_COUNT, USERS), jnp.float32) ** steps_of(splits[4], (POOL_CELL_COUNT, USERS), ((0, 32),), -0.2, 0.2)), 0.25, 4.0)
    neighbours = draw_neighbours(jax.random.fold_in(splits[7], 71), 0)
    coupling = jnp.clip(jnp.exp(jax.random.uniform(splits[6], (POOL_CELL_COUNT, NEIGH), jnp.float32, math.log(0.05), math.log(0.5))), 0.05, 0.5)
    return {"channel": channel, "symbols": symbols, "layers": layers, "user_ids": user_ids, "user_power": user_power, "neighbours": neighbours, "coupling": coupling}


NORM_EPS = 1e-06
NOISE_FLOOR = 0.05
HIGHEST = lax.Precision.HIGHEST

def mix(form, left, right):
    return jnp.einsum(form, left, right, precision=HIGHEST)

def solve_cell(packed):
    chan, symbol_block, granted, amplitude, sigma = packed
    masked = chan * granted[None, None, :, :]
    chan_re = masked[:, 0]
    chan_im = masked[:, 1]
    gram_re = mix('alp,amp->lmp', chan_re, chan_re) + mix('alp,amp->lmp', chan_im, chan_im)
    gram_im = mix('alp,amp->lmp', chan_im, chan_re) - mix('alp,amp->lmp', chan_re, chan_im)
    identity = jnp.eye(MAX_LAYERS, dtype=jnp.float32)[:, :, None]
    reg_re = gram_re + identity * sigma[None, None, :]
    trace = lax.optimization_barrier(jnp.sum(jnp.diagonal(reg_re, axis1=0, axis2=1), axis=-1))
    inv_re = identity / trace[None, None, :]
    inv_im = jnp.zeros_like(inv_re)
    for iteration in range(NS_STEPS):
        prod_re = mix('lkp,kmp->lmp', reg_re, inv_re) - mix('lkp,kmp->lmp', gram_im, inv_im)
        prod_im = mix('lkp,kmp->lmp', reg_re, inv_im) + mix('lkp,kmp->lmp', gram_im, inv_re)
        fix_re = 2.0 * identity - prod_re
        fix_im = -prod_im
        next_re = mix('lkp,kmp->lmp', inv_re, fix_re) - mix('lkp,kmp->lmp', inv_im, fix_im)
        next_im = mix('lkp,kmp->lmp', inv_re, fix_im) + mix('lkp,kmp->lmp', inv_im, fix_re)
        inv_re, inv_im = (next_re, next_im)
    prec_re = mix('amp,mlp->alp', chan_re, inv_re) + mix('amp,mlp->alp', chan_im, inv_im)
    prec_im = mix('amp,mlp->alp', chan_re, inv_im) - mix('amp,mlp->alp', chan_im, inv_re)
    energy = lax.optimization_barrier(jnp.sum(prec_re * prec_re + prec_im * prec_im, axis=0))
    scale = amplitude / jnp.sqrt(energy + NORM_EPS)
    weights = jnp.stack([prec_re * scale[None], prec_im * scale[None]], 1).astype(jnp.bfloat16)
    weight_wide = weights.astype(jnp.float32)
    shaped = symbol_block.astype(jnp.float32).reshape(MAX_LAYERS, 2, SYMS, PRBS, SUBC)
    grid_re = jnp.einsum('alp,lspk->aspk', weight_wide[:, 0], shaped[:, 0]) - jnp.einsum('alp,lspk->aspk', weight_wide[:, 1], shaped[:, 1])
    grid_im = jnp.einsum('alp,lspk->aspk', weight_wide[:, 0], shaped[:, 1]) + jnp.einsum('alp,lspk->aspk', weight_wide[:, 1], shaped[:, 0])
    grid = lax.complex(grid_re, grid_im).reshape(TX_ANTENNA_COUNT, SYMS, SUBCARRIERS)
    half = SUBCARRIERS // 2
    filler = jnp.zeros((TX_ANTENNA_COUNT, SYMS, NFFT - SUBCARRIERS), grid.dtype)
    spectrum = jnp.concatenate([grid[..., half:], filler, grid[..., :half]], axis=-1)
    samples = jnp.fft.ifft(spectrum, axis=-1) * math.sqrt(NFFT)
    return jnp.stack([jnp.real(samples), jnp.imag(samples)], 1).astype(jnp.float32)

def reference(channel, symbols, layers, user_ids, user_power, neighbours, coupling):
    layer_iota = jnp.arange(MAX_LAYERS, dtype=jnp.int32)
    granted = (layer_iota[None, :, None] < layers[:, None, :]).astype(jnp.float32)
    cell_index = jnp.arange(POOL_CELL_COUNT, dtype=jnp.int32)
    power = user_power[cell_index[:, None, None], user_ids]
    amplitude = granted * jnp.sqrt(power)
    transmit = lax.optimization_barrier(jnp.sum(amplitude * amplitude, axis=1)) / MAX_LAYERS
    adjacency = lax.optimization_barrier(jnp.sum(jnp.where(neighbours[:, :, None] == cell_index[None, None, :], coupling[:, :, None], 0.0), axis=1))
    sigma = NOISE_FLOOR + jnp.dot(adjacency, transmit, precision=HIGHEST)
    return lax.map(solve_cell, (channel, symbols, granted, amplitude, sigma))
```

```python
import functools
import math

import jax
import jax.numpy as jnp
import numpy as np
from jax import lax
from jax.experimental import pallas as pl
from jax.experimental.pallas import tpu as pltpu
from jax.sharding import PartitionSpec as P

MESH = pl.DeviceIdType.MESH
NFFT = 4096
PRBS = 256
SUBC = 12
SYMS = 2
LAYERS = 16
NORM_EPS = 1e-06
NOISE_FLOOR = 0.05
LANES = 8
W = 128
F32 = jnp.float32
BF16 = jnp.bfloat16


def lanes_of(shape):
    return lax.broadcasted_iota(jnp.int32, shape, len(shape) - 1)


def swap4(x):
    lane = lanes_of(x[0].shape)
    low_half = lane < 64
    even = lax.rem(lane, 64) < 32
    y0 = jnp.where(low_half, x[0], pltpu.roll(x[2], 64, 1))
    y2 = jnp.where(low_half, pltpu.roll(x[0], 64, 1), x[2])
    y1 = jnp.where(low_half, x[1], pltpu.roll(x[3], 64, 1))
    y3 = jnp.where(low_half, pltpu.roll(x[1], 64, 1), x[3])
    z0 = jnp.where(even, y0, pltpu.roll(y1, 32, 1))
    z1 = jnp.where(even, pltpu.roll(y0, 96, 1), y1)
    z2 = jnp.where(even, y2, pltpu.roll(y3, 32, 1))
    z3 = jnp.where(even, pltpu.roll(y2, 96, 1), y3)
    return [z0, z1, z2, z3]


def pick4(x):
    lane = lanes_of(x[0].shape)
    return jnp.where(
        lane < 64,
        jnp.where(lane < 32, x[0], x[1]),
        jnp.where(lane < 96, x[2], x[3]),
    )


def spread4(x):
    r = [x, pltpu.roll(x, 32, 1), pltpu.roll(x, 64, 1), pltpu.roll(x, 96, 1)]
    return [pick4([r[(h - g) % 4] for h in range(4)]) for g in range(4)]


def total4(x):
    x = x + pltpu.roll(x, 64, 1)
    return x + pltpu.roll(x, 32, 1)


def solve_kernel(
    cells, ch, lay, uid, power, neigh, coup, w_out,
    sb, rb, amp, tx_own, tx_all, ea, ecol, scol, vs, wsb,
    hs, hr, ts, tr, ws, wr,
):
    me = lax.axis_index("lane")
    mc = lax.axis_index("cell")
    barrier = pltpu.get_barrier_semaphore()

    def lane_peer(d):
        return lax.rem(me + d, LANES)

    def cell_peer(d):
        return lax.rem(mc + d, cells)

    def greet_lane(d, _):
        pl.semaphore_signal(barrier, inc=1, device_id={"lane": lane_peer(d)}, device_id_type=MESH)
        return _

    def greet_cell(d, _):
        pl.semaphore_signal(barrier, inc=1, device_id={"cell": cell_peer(d)}, device_id_type=MESH)
        return _

    lax.fori_loop(1, LANES, greet_lane, 0)
    lax.fori_loop(1, cells, greet_cell, 0)

    root = jnp.broadcast_to(jnp.sqrt(power[...]), (LAYERS, W))
    layer = lax.broadcasted_iota(jnp.int32, (LAYERS, W), 0)
    for h in range(2):
        part = slice(h * W, (h + 1) * W)
        picked = jnp.take_along_axis(root, uid[:, part], axis=1, mode="promise_in_bounds")
        granted = layer < lay[:, part]
        spread = swap4([jnp.where(granted, picked, 0.0)] * 4)
        for q in range(4):
            amp[4 * h + q] = spread[q]
        mask = jnp.where(granted, 1.0, 0.0)
        for ah in range(2):
            for c in range(2):
                turned = swap4([ch[ah * 4 + g, c, :, part] * mask for g in range(4)])
                for q in range(4):
                    sb[2 * (4 * h + q) + ah, c] = turned[q]
    own_amp = amp[me]
    transmit = jnp.sum(own_amp * own_amp, axis=0, keepdims=True) / LAYERS
    tx_own[...] = transmit
    tx_all[mc] = transmit

    def tx_copy(d):
        return pltpu.make_async_remote_copy(
            src_ref=tx_own, dst_ref=tx_all.at[mc], send_sem=ts.at[d - 1], recv_sem=tr.at[d - 1],
            device_id={"cell": cell_peer(d)}, device_id_type=MESH,
        )

    def block_copy(src, dst, send, recv, d):
        return pltpu.make_async_remote_copy(
            src_ref=src.at[pl.ds(2 * lane_peer(d), 2)], dst_ref=dst.at[pl.ds(2 * me, 2)],
            send_sem=send.at[d - 1], recv_sem=recv.at[d - 1],
            device_id={"lane": lane_peer(d)}, device_id_type=MESH,
        )

    far_first = (4, 3, 5, 2, 6, 1, 7)
    pl.semaphore_wait(barrier, LANES - 1 + cells - 1)
    for d in far_first:
        block_copy(sb, rb, hs, hr, d).start()

    def start_tx(d, _):
        tx_copy(d).start()
        return _

    lax.fori_loop(1, cells, start_tx, 0)
    rb[pl.ds(2 * me, 2)] = sb[pl.ds(2 * me, 2)]

    def end_tx(d, _):
        tx_copy(d).wait()
        return _

    lax.fori_loop(1, cells, end_tx, 0)
    sigma = jnp.full((1, W), NOISE_FLOOR, F32)
    for k in range(neigh.shape[1]):
        sigma = sigma + coup[mc, k] * tx_all[neigh[mc, k]]
    for d in far_first[::-1]:
        block_copy(sb, rb, hs, hr, d).wait()

    zero = jnp.zeros((8, W), F32)
    for lt in range(2):
        rows = slice(8 * lt, 8 * lt + 8)

        def gram_step(a, acc, rows=rows):
            ar, ai = rb[a, 0, rows, :], rb[a, 1, rows, :]
            out = []
            for m in range(LAYERS):
                br, bi = rb[a, 0, m : m + 1, :], rb[a, 1, m : m + 1, :]
                out.append(acc[2 * m] + (ar * br + ai * bi))
                out.append(acc[2 * m + 1] + (ai * br - ar * bi))
            return tuple(out)

        acc = lax.fori_loop(0, 2 * LANES, gram_step, (zero,) * (2 * LAYERS))
        for m in range(LAYERS):
            ea[0, m, rows, :] = total4(acc[2 * m])
            ea[1, m, rows, :] = total4(acc[2 * m + 1])

    diagonal = jnp.zeros((LAYERS, W), F32)
    for m in range(LAYERS):
        diagonal = diagonal + jnp.where(layer == m, ea[0, m] + sigma, 0.0)
    inv_trace = 1.0 / jnp.sum(diagonal, axis=0, keepdims=True)
    for m in range(LAYERS):
        ea[0, m] = jnp.where(layer == m, 1.0 - (ea[0, m] + sigma) * inv_trace, -ea[0, m] * inv_trace)
        ea[1, m] = -ea[1, m] * inv_trace
    column = lanes_of((LAYERS, W)) // 32
    for j in range(4):
        for c in range(2):
            ecol[c, j] = pick4([ea[c, 4 * j + g] for g in range(4)])
        scol[0, j] = ecol[0, j] + jnp.where(layer == 4 * j + column, 1.0, 0.0)
        scol[1, j] = ecol[1, j]

    def products(refs):
        sums = [[[jnp.zeros((LAYERS, W), F32) for j in range(4)] for c in range(2)] for _ in refs]
        for k in range(LAYERS):
            ar, ai = ea[0, k], ea[1, k]
            for out, ref in zip(sums, refs):
                for j in range(4):
                    br, bi = ref[0, j, k : k + 1, :], ref[1, j, k : k + 1, :]
                    out[0][j] = out[0][j] + (ar * br - ai * bi)
                    out[1][j] = out[1][j] + (ar * bi + ai * br)
        return sums

    def put_square(square):
        for c in range(2):
            for j in range(4):
                ecol[c, j] = square[c][j]
                full = spread4(square[c][j])
                for g in range(4):
                    ea[c, 4 * j + g] = full[g]

    put_square(products([ecol])[0])

    def level(i, _):
        square, more = products([ecol, scol])
        for c in range(2):
            for j in range(4):
                scol[c, j] = scol[c, j] + more[c][j]
        put_square(square)
        return _

    lax.fori_loop(1, 5, level, 0)
    (more,) = products([scol])
    for c in range(2):
        for j in range(4):
            full = spread4((scol[c, j] + more[c][j]) * inv_trace)
            for g in range(4):
                ea[c, 4 * j + g] = full[g]

    def apply_step(z, energy):
        sums = [[jnp.zeros((LAYERS, W), F32) for c in range(2)] for ah in range(2)]
        for m in range(LAYERS):
            xr, xi = ea[0, m], ea[1, m]
            for ah in range(2):
                br, bi = rb[2 * z + ah, 0, m : m + 1, :], rb[2 * z + ah, 1, m : m + 1, :]
                sums[ah][0] = sums[ah][0] + (br * xr - bi * xi)
                sums[ah][1] = sums[ah][1] + (br * xi + bi * xr)
        for ah in range(2):
            vr, vi = sums[ah]
            vs[2 * z + ah, 0] = vr
            vs[2 * z + ah, 1] = -vi
            energy = energy + (vr * vr + vi * vi)
        return energy

    energy = total4(lax.fori_loop(0, LANES, apply_step, jnp.zeros((LAYERS, W), F32)))
    scale = own_amp / jnp.sqrt(energy + NORM_EPS)

    def round_step(a, _):
        for c in range(2):
            wsb[a, c] = (vs[a, c] * scale).astype(BF16)
        return _

    lax.fori_loop(0, 2 * LANES, round_step, 0)
    for d in far_first:
        block_copy(wsb, w_out, ws, wr, d).start()
    w_out[pl.ds(2 * me, 2)] = wsb[pl.ds(2 * me, 2)]
    for d in far_first[::-1]:
        block_copy(wsb, w_out, ws, wr, d).wait()


def solve(cells, channel, layers, user_ids, user_power, neighbours, coupling):
    vmem = pl.BlockSpec(memory_space=pltpu.VMEM)
    smem = pl.BlockSpec(memory_space=pltpu.SMEM)
    block = (2 * LANES, 2, LAYERS, W)
    dma = pltpu.SemaphoreType.DMA
    return pl.pallas_call(
        functools.partial(solve_kernel, cells),
        out_shape=jax.ShapeDtypeStruct(block, BF16),
        in_specs=[vmem] * 4 + [smem] * 2,
        out_specs=vmem,
        scratch_shapes=[
            pltpu.VMEM(block, F32),
            pltpu.VMEM(block, F32),
            pltpu.VMEM((LANES, LAYERS, W), F32),
            pltpu.VMEM((1, W), F32),
            pltpu.VMEM((cells, 1, W), F32),
            pltpu.VMEM((2, LAYERS, LAYERS, W), F32),
            pltpu.VMEM((2, 4, LAYERS, W), F32),
            pltpu.VMEM((2, 4, LAYERS, W), F32),
            pltpu.VMEM(block, F32),
            pltpu.VMEM(block, BF16),
            dma((LANES - 1,)),
            dma((LANES - 1,)),
            dma((cells - 1,)),
            dma((cells - 1,)),
            dma((LANES - 1,)),
            dma((LANES - 1,)),
        ],
        compiler_params=pltpu.CompilerParams(collective_id=0, has_side_effects=True),
        name="solve",
    )(channel, layers, user_ids, user_power, neighbours, coupling)


def ofdm_kernel(w, sym, dft, twist, out, tmp, sy, wn, gf, lhs):
    j = lax.broadcasted_iota(jnp.int32, (384, 384), 0)
    o = lax.broadcasted_iota(jnp.int32, (384, 384), 1)
    source = SUBC * lax.rem(o, 32) + o // 32
    order = jnp.where(j == source, 1.0, 0.0).astype(BF16)
    for z in range(8):
        tmp[z] = jnp.dot(sym[:, 384 * z : 384 * (z + 1)], order, preferred_element_type=F32)
    for h in range(2):
        for t in range(3):
            turned = swap4([tmp[4 * h + q, :, W * t : W * (t + 1)] for q in range(4)])
            for kk in range(4):
                k = 4 * t + kk
                for s in range(SYMS):
                    for b in range(4):
                        sy[h, pl.ds(b * 8 * 24 + s * SUBC + k, 8, stride=24), :] = turned[kk][
                            s * 32 + b * 8 : s * 32 + b * 8 + 8, :
                        ]
        for ah in range(2):
            for c in range(2):
                turned = swap4([w[2 * (4 * h + q) + ah, c].astype(F32) for q in range(4)])
                for g in range(4):
                    wn[h, ah * 4 + g, c] = turned[g]

    for h in range(2):

        def precode(half, _, h=h):
            sums = [[[jnp.zeros((8, W), F32) for i in range(3)] for c in range(2)] for a in range(4)]
            for l in range(LAYERS):
                sr = [sy[h, (2 * l) * 24 + 8 * i : (2 * l) * 24 + 8 * i + 8, :] for i in range(3)]
                si = [sy[h, (2 * l + 1) * 24 + 8 * i : (2 * l + 1) * 24 + 8 * i + 8, :] for i in range(3)]
                for a in range(4):
                    wr = wn[h, 4 * half + a, 0, l : l + 1, :]
                    wi = wn[h, 4 * half + a, 1, l : l + 1, :]
                    for i in range(3):
                        sums[a][0][i] = sums[a][0][i] + (wr * sr[i] - wi * si[i])
                        sums[a][1][i] = sums[a][1][i] + (wr * si[i] + wi * sr[i])
            for a in range(4):
                for c in range(2):
                    for i in range(3):
                        gf[c, h, pl.ds(64 * i + 4 * half + a, 8, stride=8), :] = sums[a][c][i]
            return _

        lax.fori_loop(0, 2, precode, 0)

    for c in range(2):
        for h in range(2):
            value = gf[c, h]
            high = value.astype(BF16)
            cols = slice(c * PRBS + h * W, c * PRBS + (h + 1) * W)
            lhs[0:192, cols] = high
            lhs[192:384, cols] = (value - high.astype(F32)).astype(BF16)

    def section(nt, _):
        result = jnp.dot(lhs[...], dft[nt], preferred_element_type=F32)
        result = result[0:192] + result[192:384]
        for s in range(SYMS):
            part = [[None, None] for _ in range(4)]
            for k in range(SUBC):
                row = (s * SUBC + k) * 8
                tr, ti = result[row : row + 8, 0:W], result[row : row + 8, W : 2 * W]
                cr, ci = twist[nt, k : k + 1, :], twist[nt, SUBC + k : SUBC + k + 1, :]
                ur, ui = tr * cr - ti * ci, tr * ci + ti * cr
                held = part[k % 4]
                held[0] = ur if held[0] is None else held[0] + ur
                held[1] = ui if held[1] is None else held[1] + ui
            (ar, ai), (br, bi), (cr, ci), (dr, di) = part
            pr, pi, mr, mi = ar + cr, ai + ci, ar - cr, ai - ci
            qr, qi, nr, ni = br + dr, bi + di, br - dr, bi - di
            outs = ((pr + qr, pi + qi), (mr - ni, mi + nr), (pr - qr, pi - qi), (mr + ni, mi - nr))
            for n2 in range(4):
                for c in range(2):
                    out[pl.ds(c * 64 + (n2 * 8 + nt) * 2 + s, 8, stride=128), :] = outs[n2][c]
        return _

    lax.fori_loop(0, 8, section, 0)


def ofdm_tables():
    p = np.arange(PRBS)[:, None]
    n = np.arange(1024)[None, :]
    angle = 2.0 * math.pi * ((3 * p * n) % 1024) / 1024
    cos, sin = np.cos(angle), np.sin(angle)
    real = np.concatenate([cos, -sin], 0).reshape(2 * PRBS, 8, 1, W)
    imag = np.concatenate([sin, cos], 0).reshape(2 * PRBS, 8, 1, W)
    dft = np.concatenate([real, imag], 2).reshape(2 * PRBS, 8, 2 * W).transpose(1, 0, 2)
    k = np.arange(SUBC)[:, None]
    angle = 2.0 * math.pi * (((k - 1536) * n) % NFFT) / NFFT
    twist = np.concatenate([np.cos(angle), np.sin(angle)], 0) / math.sqrt(NFFT)
    twist = twist.reshape(2 * SUBC, 8, W).transpose(1, 0, 2)
    return jnp.asarray(dft, BF16), jnp.asarray(twist, F32)


def ofdm(weights, symbols):
    vmem = pl.BlockSpec(memory_space=pltpu.VMEM)
    dft, twist = ofdm_tables()
    return pl.pallas_call(
        ofdm_kernel,
        out_shape=jax.ShapeDtypeStruct((1024, W), F32),
        in_specs=[vmem] * 4,
        out_specs=vmem,
        scratch_shapes=[
            pltpu.VMEM((8, 64, 384), F32),
            pltpu.VMEM((2, 768, W), F32),
            pltpu.VMEM((2, 8, 2, LAYERS, W), F32),
            pltpu.VMEM((2, 2, 192, W), F32),
            pltpu.VMEM((384, 512), BF16),
        ],
        name="ofdm",
    )(weights, symbols, dft, twist)


def per_device(cells, channel, symbols, layers, user_ids, user_power, neighbours, coupling):
    weights = solve(cells, channel[0], layers, user_ids[0], user_power, neighbours, coupling)
    rows = jnp.transpose(symbols[0], (2, 0, 1, 3)).reshape(64, 3072)
    samples = ofdm(weights, rows)
    samples = samples.reshape(8, 2, 32, SYMS, W).transpose(0, 1, 3, 2, 4)
    return samples.reshape(1, 8, 2, SYMS, NFFT)


def solution(mesh):
    in_specs = (
        P("cell", "lane", None, None, None),
        P("cell", None, None, None, None),
        P("cell", None),
        P("cell", None, None),
        P("cell", None),
        P(),
        P(),
    )
    out_specs = P("cell", "lane", None, None, None)
    return jax.shard_map(
        functools.partial(per_device, mesh.shape["cell"]),
        mesh=mesh, in_specs=in_specs, out_specs=out_specs, check_vma=False,
    )
```

```python
import functools
import math

import jax
import jax.numpy as jnp
import numpy as np
from jax import lax
from jax.experimental import pallas as pl
from jax.experimental.pallas import tpu as pltpu
from jax.sharding import PartitionSpec as P

MESH = pl.DeviceIdType.MESH
NFFT = 4096
PRBS = 256
SUBC = 12
SYMS = 2
LAYERS = 16
NORM_EPS = 1e-06
NOISE_FLOOR = 0.05
LANES = 8
W = 128
F32 = jnp.float32
BF16 = jnp.bfloat16


def lanes_of(shape):
    return lax.broadcasted_iota(jnp.int32, shape, len(shape) - 1)


def swap4(x):
    lane = lanes_of(x[0].shape)
    low_half = lane < 64
    even = lax.rem(lane, 64) < 32
    y0 = jnp.where(low_half, x[0], pltpu.roll(x[2], 64, 1))
    y2 = jnp.where(low_half, pltpu.roll(x[0], 64, 1), x[2])
    y1 = jnp.where(low_half, x[1], pltpu.roll(x[3], 64, 1))
    y3 = jnp.where(low_half, pltpu.roll(x[1], 64, 1), x[3])
    z0 = jnp.where(even, y0, pltpu.roll(y1, 32, 1))
    z1 = jnp.where(even, pltpu.roll(y0, 96, 1), y1)
    z2 = jnp.where(even, y2, pltpu.roll(y3, 32, 1))
    z3 = jnp.where(even, pltpu.roll(y2, 96, 1), y3)
    return [z0, z1, z2, z3]


def pick4(x):
    lane = lanes_of(x[0].shape)
    return jnp.where(
        lane < 64,
        jnp.where(lane < 32, x[0], x[1]),
        jnp.where(lane < 96, x[2], x[3]),
    )


def spread4(x):
    r = [x, pltpu.roll(x, 32, 1), pltpu.roll(x, 64, 1), pltpu.roll(x, 96, 1)]
    return [pick4([r[(h - g) % 4] for h in range(4)]) for g in range(4)]


def total4(x):
    x = x + pltpu.roll(x, 64, 1)
    return x + pltpu.roll(x, 32, 1)


def spread_symbols(sym, symf, tmp, sy):
    def widen(lc, _):
        pair = sym[lc].astype(F32)
        symf[pl.ds(lc, 1), :] = pair[0:1, :]
        symf[pl.ds(2 * LAYERS + lc, 1), :] = pair[1:2, :]
        return _

    lax.fori_loop(0, 2 * LAYERS, widen, 0)
    j = lax.broadcasted_iota(jnp.int32, (384, 384), 0)
    o = lax.broadcasted_iota(jnp.int32, (384, 384), 1)
    source = SUBC * lax.rem(o, 32) + o // 32
    order = jnp.where(j == source, 1.0, 0.0).astype(BF16)
    for z in range(8):
        tmp[z] = jnp.dot(symf[:, 384 * z : 384 * (z + 1)].astype(BF16), order, preferred_element_type=F32)
    for h in range(2):
        for t in range(3):
            turned = swap4([tmp[4 * h + q, :, W * t : W * (t + 1)] for q in range(4)])
            for kk in range(4):
                k = 4 * t + kk
                for s in range(SYMS):
                    for b in range(4):
                        sy[h, pl.ds(b * 8 * 24 + s * SUBC + k, 8, stride=24), :] = turned[kk][
                            s * 32 + b * 8 : s * 32 + b * 8 + 8, :
                        ]


def slot_kernel(
    cells, ch_any, sym_any, lay_any, uid_any, power_any, neigh_any, coup_any, dft_any, twist_any, out,
    ch, sym, lay, uid, power, neigh, coup, dft, twist,
    sb, rb, amp, tx_own, tx_all, ea, ecol, scol, vs, wsb, w_out,
    symf, tmp, sy, wn, gf, lhs,
    ins, hs, hr, ts, tr, ws, wr,
):
    fetches = [
        pltpu.make_async_copy(source, held, ins.at[i])
        for i, (source, held) in enumerate((
            (lay_any, lay), (uid_any, uid), (power_any, power), (ch_any, ch), (neigh_any, neigh),
            (coup_any, coup), (sym_any, sym), (dft_any, dft), (twist_any, twist),
        ))
    ]
    for fetch in fetches:
        fetch.start()
    me = lax.axis_index("lane")
    mc = lax.axis_index("cell")
    barrier = pltpu.get_barrier_semaphore()

    def lane_peer(d):
        return lax.rem(me + d, LANES)

    def cell_peer(d):
        return lax.rem(mc + d, cells)

    def greet_lane(d, _):
        pl.semaphore_signal(barrier, inc=1, device_id={"lane": lane_peer(d)}, device_id_type=MESH)
        return _

    def greet_cell(d, _):
        pl.semaphore_signal(barrier, inc=1, device_id={"cell": cell_peer(d)}, device_id_type=MESH)
        return _

    lax.fori_loop(1, LANES, greet_lane, 0)
    lax.fori_loop(1, cells, greet_cell, 0)

    for fetch in fetches[:4]:
        fetch.wait()
    root = jnp.broadcast_to(jnp.sqrt(power[...]), (LAYERS, W))
    layer = lax.broadcasted_iota(jnp.int32, (LAYERS, W), 0)
    for h in range(2):
        part = slice(h * W, (h + 1) * W)
        picked = jnp.take_along_axis(root, uid[:, part], axis=1, mode="promise_in_bounds")
        granted = layer < lay[:, part]
        spread = swap4([jnp.where(granted, picked, 0.0)] * 4)
        for q in range(4):
            amp[4 * h + q] = spread[q]
        mask = jnp.where(granted, 1.0, 0.0)
        for ah in range(2):
            for c in range(2):
                turned = swap4([ch[ah * 4 + g, c, :, part] * mask for g in range(4)])
                for q in range(4):
                    sb[2 * (4 * h + q) + ah, c] = turned[q]
    own_amp = amp[me]
    transmit = jnp.sum(own_amp * own_amp, axis=0, keepdims=True) / LAYERS
    tx_own[...] = transmit
    tx_all[mc] = transmit

    def tx_copy(d):
        return pltpu.make_async_remote_copy(
            src_ref=tx_own, dst_ref=tx_all.at[mc], send_sem=ts.at[d - 1], recv_sem=tr.at[d - 1],
            device_id={"cell": cell_peer(d)}, device_id_type=MESH,
        )

    def block_copy(src, dst, send, recv, d):
        return pltpu.make_async_remote_copy(
            src_ref=src.at[pl.ds(2 * lane_peer(d), 2)], dst_ref=dst.at[pl.ds(2 * me, 2)],
            send_sem=send.at[d - 1], recv_sem=recv.at[d - 1],
            device_id={"lane": lane_peer(d)}, device_id_type=MESH,
        )

    far_first = (4, 3, 5, 2, 6, 1, 7)
    pl.semaphore_wait(barrier, LANES - 1 + cells - 1)
    for d in far_first:
        block_copy(sb, rb, hs, hr, d).start()

    def start_tx(d, _):
        tx_copy(d).start()
        return _

    lax.fori_loop(1, cells, start_tx, 0)
    rb[pl.ds(2 * me, 2)] = sb[pl.ds(2 * me, 2)]

    fetches[6].wait()
    spread_symbols(sym, symf, tmp, sy)

    def end_tx(d, _):
        tx_copy(d).wait()
        return _

    lax.fori_loop(1, cells, end_tx, 0)
    fetches[4].wait()
    fetches[5].wait()
    sigma = jnp.full((1, W), NOISE_FLOOR, F32)
    for k in range(neigh.shape[0]):
        sigma = sigma + coup[k, mc] * tx_all[neigh[k, mc]]
    for d in far_first[::-1]:
        block_copy(sb, rb, hs, hr, d).wait()

    zero = jnp.zeros((8, W), F32)
    for lt in range(2):
        rows = slice(8 * lt, 8 * lt + 8)

        def gram_step(a, acc, rows=rows):
            ar, ai = rb[a, 0, rows, :], rb[a, 1, rows, :]
            out = []
            for m in range(LAYERS):
                br, bi = rb[a, 0, m : m + 1, :], rb[a, 1, m : m + 1, :]
                out.append(acc[2 * m] + (ar * br + ai * bi))
                out.append(acc[2 * m + 1] + (ai * br - ar * bi))
            return tuple(out)

        acc = lax.fori_loop(0, 2 * LANES, gram_step, (zero,) * (2 * LAYERS))
        for m in range(LAYERS):
            ea[0, m, rows, :] = total4(acc[2 * m])
            ea[1, m, rows, :] = total4(acc[2 * m + 1])

    diagonal = jnp.zeros((LAYERS, W), F32)
    for m in range(LAYERS):
        diagonal = diagonal + jnp.where(layer == m, ea[0, m] + sigma, 0.0)
    inv_trace = 1.0 / jnp.sum(diagonal, axis=0, keepdims=True)
    for m in range(LAYERS):
        ea[0, m] = jnp.where(layer == m, 1.0 - (ea[0, m] + sigma) * inv_trace, -ea[0, m] * inv_trace)
        ea[1, m] = -ea[1, m] * inv_trace
    column = lanes_of((LAYERS, W)) // 32
    for j in range(4):
        for c in range(2):
            ecol[c, j] = pick4([ea[c, 4 * j + g] for g in range(4)])
        scol[0, j] = ecol[0, j] + jnp.where(layer == 4 * j + column, 1.0, 0.0)
        scol[1, j] = ecol[1, j]

    def products(refs):
        sums = [[[jnp.zeros((LAYERS, W), F32) for j in range(4)] for c in range(2)] for _ in refs]
        for k in range(LAYERS):
            ar, ai = ea[0, k], ea[1, k]
            for out, ref in zip(sums, refs):
                for j in range(4):
                    br, bi = ref[0, j, k : k + 1, :], ref[1, j, k : k + 1, :]
                    out[0][j] = out[0][j] + (ar * br - ai * bi)
                    out[1][j] = out[1][j] + (ar * bi + ai * br)
        return sums

    def put_square(square):
        for c in range(2):
            for j in range(4):
                ecol[c, j] = square[c][j]
                full = spread4(square[c][j])
                for g in range(4):
                    ea[c, 4 * j + g] = full[g]

    put_square(products([ecol])[0])

    def level(i, _):
        square, more = products([ecol, scol])
        for c in range(2):
            for j in range(4):
                scol[c, j] = scol[c, j] + more[c][j]
        put_square(square)
        return _

    lax.fori_loop(1, 5, level, 0)
    (more,) = products([scol])
    for c in range(2):
        for j in range(4):
            full = spread4((scol[c, j] + more[c][j]) * inv_trace)
            for g in range(4):
                ea[c, 4 * j + g] = full[g]

    def apply_step(z, energy):
        sums = [[jnp.zeros((LAYERS, W), F32) for c in range(2)] for ah in range(2)]
        for m in range(LAYERS):
            xr, xi = ea[0, m], ea[1, m]
            for ah in range(2):
                br, bi = rb[2 * z + ah, 0, m : m + 1, :], rb[2 * z + ah, 1, m : m + 1, :]
                sums[ah][0] = sums[ah][0] + (br * xr - bi * xi)
                sums[ah][1] = sums[ah][1] + (br * xi + bi * xr)
        for ah in range(2):
            vr, vi = sums[ah]
            vs[2 * z + ah, 0] = vr
            vs[2 * z + ah, 1] = -vi
            energy = energy + (vr * vr + vi * vi)
        return energy

    energy = total4(lax.fori_loop(0, LANES, apply_step, jnp.zeros((LAYERS, W), F32)))
    scale = own_amp / jnp.sqrt(energy + NORM_EPS)

    def round_step(a, _):
        for c in range(2):
            wsb[a, c] = (vs[a, c] * scale).astype(BF16)
        return _

    lax.fori_loop(0, 2 * LANES, round_step, 0)
    for d in far_first:
        block_copy(wsb, w_out, ws, wr, d).start()
    w_out[pl.ds(2 * me, 2)] = wsb[pl.ds(2 * me, 2)]
    for d in far_first[::-1]:
        block_copy(wsb, w_out, ws, wr, d).wait()

    for h in range(2):
        for ah in range(2):
            for c in range(2):
                turned = swap4([w_out[2 * (4 * h + q) + ah, c].astype(F32) for q in range(4)])
                for g in range(4):
                    wn[h, ah * 4 + g, c] = turned[g]

    for h in range(2):

        def precode(half, _, h=h):
            sums = [[[jnp.zeros((8, W), F32) for i in range(3)] for c in range(2)] for a in range(4)]
            for l in range(LAYERS):
                sr = [sy[h, (2 * l) * 24 + 8 * i : (2 * l) * 24 + 8 * i + 8, :] for i in range(3)]
                si = [sy[h, (2 * l + 1) * 24 + 8 * i : (2 * l + 1) * 24 + 8 * i + 8, :] for i in range(3)]
                for a in range(4):
                    wr = wn[h, 4 * half + a, 0, l : l + 1, :]
                    wi = wn[h, 4 * half + a, 1, l : l + 1, :]
                    for i in range(3):
                        sums[a][0][i] = sums[a][0][i] + (wr * sr[i] - wi * si[i])
                        sums[a][1][i] = sums[a][1][i] + (wr * si[i] + wi * sr[i])
            for a in range(4):
                for c in range(2):
                    for i in range(3):
                        gf[c, h, pl.ds(64 * i + 4 * half + a, 8, stride=8), :] = sums[a][c][i]
            return _

        lax.fori_loop(0, 2, precode, 0)

    for c in range(2):
        for h in range(2):
            value = gf[c, h]
            high = value.astype(BF16)
            cols = slice(c * PRBS + h * W, c * PRBS + (h + 1) * W)
            lhs[0:192, cols] = high
            lhs[192:384, cols] = (value - high.astype(F32)).astype(BF16)

    fetches[7].wait()
    fetches[8].wait()

    def section(nt, _):
        result = jnp.dot(lhs[...], dft[nt], preferred_element_type=F32)
        result = result[0:192] + result[192:384]
        for s in range(SYMS):
            part = [[None, None] for _ in range(4)]
            for k in range(SUBC):
                row = (s * SUBC + k) * 8
                tr, ti = result[row : row + 8, 0:W], result[row : row + 8, W : 2 * W]
                cr, ci = twist[nt, k : k + 1, :], twist[nt, SUBC + k : SUBC + k + 1, :]
                ur, ui = tr * cr - ti * ci, tr * ci + ti * cr
                held = part[k % 4]
                held[0] = ur if held[0] is None else held[0] + ur
                held[1] = ui if held[1] is None else held[1] + ui
            (ar, ai), (br, bi), (cr, ci), (dr, di) = part
            pr, pi, mr, mi = ar + cr, ai + ci, ar - cr, ai - ci
            qr, qi, nr, ni = br + dr, bi + di, br - dr, bi - di
            outs = ((pr + qr, pi + qi), (mr - ni, mi + nr), (pr - qr, pi - qi), (mr + ni, mi - nr))
            for n2 in range(4):
                for c in range(2):
                    out[pl.ds(c * 64 + (n2 * 8 + nt) * 2 + s, 8, stride=128), :] = outs[n2][c]
        return _

    lax.fori_loop(0, 8, section, 0)


def ofdm_tables():
    p = np.arange(PRBS)[:, None]
    n = np.arange(1024)[None, :]
    angle = 2.0 * math.pi * ((3 * p * n) % 1024) / 1024
    cos, sin = np.cos(angle), np.sin(angle)
    real = np.concatenate([cos, -sin], 0).reshape(2 * PRBS, 8, 1, W)
    imag = np.concatenate([sin, cos], 0).reshape(2 * PRBS, 8, 1, W)
    dft = np.concatenate([real, imag], 2).reshape(2 * PRBS, 8, 2 * W).transpose(1, 0, 2)
    k = np.arange(SUBC)[:, None]
    angle = 2.0 * math.pi * (((k - 1536) * n) % NFFT) / NFFT
    twist = np.concatenate([np.cos(angle), np.sin(angle)], 0) / math.sqrt(NFFT)
    twist = twist.reshape(2 * SUBC, 8, W).transpose(1, 0, 2)
    return jnp.asarray(dft, BF16), jnp.asarray(twist, F32)


def slot(cells, channel, symbols, layers, user_ids, user_power, neighbours, coupling):
    dft, twist = ofdm_tables()
    args = (channel, symbols, layers, user_ids, user_power, neighbours, coupling, dft, twist)
    block = (2 * LANES, 2, LAYERS, W)
    dma = pltpu.SemaphoreType.DMA
    held = [(pltpu.SMEM if i in (5, 6) else pltpu.VMEM)(x.shape, x.dtype) for i, x in enumerate(args)]
    return pl.pallas_call(
        functools.partial(slot_kernel, cells),
        out_shape=jax.ShapeDtypeStruct((1024, W), F32),
        in_specs=[pl.BlockSpec(memory_space=pl.ANY)] * len(args),
        out_specs=pl.BlockSpec(memory_space=pltpu.VMEM),
        scratch_shapes=held + [
            pltpu.VMEM(block, F32),
            pltpu.VMEM(block, F32),
            pltpu.VMEM((LANES, LAYERS, W), F32),
            pltpu.VMEM((1, W), F32),
            pltpu.VMEM((cells, 1, W), F32),
            pltpu.VMEM((2, LAYERS, LAYERS, W), F32),
            pltpu.VMEM((2, 4, LAYERS, W), F32),
            pltpu.VMEM((2, 4, LAYERS, W), F32),
            pltpu.VMEM(block, F32),
            pltpu.VMEM(block, BF16),
            pltpu.VMEM(block, BF16),
            pltpu.VMEM((64, 3072), F32),
            pltpu.VMEM((8, 64, 384), F32),
            pltpu.VMEM((2, 768, W), F32),
            pltpu.VMEM((2, 8, 2, LAYERS, W), F32),
            pltpu.VMEM((2, 2, 192, W), F32),
            pltpu.VMEM((384, 512), BF16),
            dma((len(args),)),
            dma((LANES - 1,)),
            dma((LANES - 1,)),
            dma((cells - 1,)),
            dma((cells - 1,)),
            dma((LANES - 1,)),
            dma((LANES - 1,)),
        ],
        compiler_params=pltpu.CompilerParams(collective_id=0, has_side_effects=True),
        name="slot",
    )(*args)


def per_device(cells, channel, symbols, layers, user_ids, user_power, neighbours, coupling):
    samples = slot(
        cells, channel[0], symbols[0].reshape(2 * LAYERS, SYMS, 3072), layers, user_ids[0], user_power,
        neighbours.T, coupling.T,
    )
    samples = samples.reshape(8, 2, 32, SYMS, W).transpose(0, 1, 3, 2, 4)
    return samples.reshape(1, 8, 2, SYMS, NFFT)


def solution(mesh):
    in_specs = (
        P("cell", "lane", None, None, None),
        P("cell", None, None, None, None),
        P("cell", None),
        P("cell", None, None),
        P("cell", None),
        P(),
        P(),
    )
    out_specs = P("cell", "lane", None, None, None)
    return jax.shard_map(
        functools.partial(per_device, mesh.shape["cell"]),
        mesh=mesh, in_specs=in_specs, out_specs=out_specs, check_vma=False,
    )
```

```python
import functools
import math

import jax
import jax.numpy as jnp
import numpy as np
from jax import lax
from jax.experimental import pallas as pl
from jax.experimental.pallas import tpu as pltpu
from jax.sharding import PartitionSpec as P

MESH = pl.DeviceIdType.MESH
NFFT = 4096
PRBS = 256
SUBC = 12
SYMS = 2
LAYERS = 16
NORM_EPS = 1e-06
NOISE_FLOOR = 0.05
LANES = 8
W = 128
F32 = jnp.float32
BF16 = jnp.bfloat16


def lanes_of(shape):
    return lax.broadcasted_iota(jnp.int32, shape, len(shape) - 1)


def swap4(x):
    lane = lanes_of(x[0].shape)
    low_half = lane < 64
    even = lax.rem(lane, 64) < 32
    y0 = jnp.where(low_half, x[0], pltpu.roll(x[2], 64, 1))
    y2 = jnp.where(low_half, pltpu.roll(x[0], 64, 1), x[2])
    y1 = jnp.where(low_half, x[1], pltpu.roll(x[3], 64, 1))
    y3 = jnp.where(low_half, pltpu.roll(x[1], 64, 1), x[3])
    z0 = jnp.where(even, y0, pltpu.roll(y1, 32, 1))
    z1 = jnp.where(even, pltpu.roll(y0, 96, 1), y1)
    z2 = jnp.where(even, y2, pltpu.roll(y3, 32, 1))
    z3 = jnp.where(even, pltpu.roll(y2, 96, 1), y3)
    return [z0, z1, z2, z3]


def pick4(x):
    lane = lanes_of(x[0].shape)
    return jnp.where(
        lane < 64,
        jnp.where(lane < 32, x[0], x[1]),
        jnp.where(lane < 96, x[2], x[3]),
    )


def spread4(x):
    r = [x, pltpu.roll(x, 32, 1), pltpu.roll(x, 64, 1), pltpu.roll(x, 96, 1)]
    return [pick4([r[(h - g) % 4] for h in range(4)]) for g in range(4)]


def total4(x):
    x = x + pltpu.roll(x, 64, 1)
    return x + pltpu.roll(x, 32, 1)


def spread_symbols(sym, symf, tmp, sy):
    def widen(lc, _):
        pair = sym[lc].astype(F32)
        symf[pl.ds(lc, 1), :] = pair[0:1, :]
        symf[pl.ds(2 * LAYERS + lc, 1), :] = pair[1:2, :]
        return _

    lax.fori_loop(0, 2 * LAYERS, widen, 0)
    j = lax.broadcasted_iota(jnp.int32, (384, 384), 0)
    o = lax.broadcasted_iota(jnp.int32, (384, 384), 1)
    source = SUBC * lax.rem(o, 32) + o // 32
    order = jnp.where(j == source, 1.0, 0.0).astype(BF16)
    for z in range(8):
        tmp[z] = jnp.dot(symf[:, 384 * z : 384 * (z + 1)].astype(BF16), order, preferred_element_type=F32)
    for h in range(2):
        for t in range(3):
            turned = swap4([tmp[4 * h + q, :, W * t : W * (t + 1)] for q in range(4)])
            for kk in range(4):
                k = 4 * t + kk
                for s in range(SYMS):
                    for b in range(4):
                        sy[h, pl.ds(b * 8 * 24 + s * SUBC + k, 8, stride=24), :] = turned[kk][
                            s * 32 + b * 8 : s * 32 + b * 8 + 8, :
                        ]


def slot_kernel(
    cells, ch_any, sym_any, lay_any, uid_any, power_any, neigh_any, coup_any, dft_any, twist_any, out,
    ch, sym, lay, uid, power, neigh, coup, dft, twist,
    sb, rb, amp, tx_own, tx_all, sig_all, sig_in, ea, ecol, scol, vs, wsb, w_out,
    symf, tmp, sy, wn, gf, lhs,
    ins, hs, hr, ts, tr, ss, sr, ws, wr,
):
    fetches = [
        pltpu.make_async_copy(source, held, ins.at[i])
        for i, (source, held) in enumerate((
            (lay_any, lay), (uid_any, uid), (power_any, power), (ch_any, ch), (neigh_any, neigh),
            (coup_any, coup), (sym_any, sym), (dft_any, dft), (twist_any, twist),
        ))
    ]
    for fetch in fetches:
        fetch.start()
    me = lax.axis_index("lane")
    mc = lax.axis_index("cell")
    barrier = pltpu.get_barrier_semaphore()

    def lane_peer(d):
        return lax.rem(me + d, LANES)

    def cell_peer(d):
        return lax.rem(mc + d, cells)

    def greet_lane(d, _):
        pl.semaphore_signal(barrier, inc=1, device_id={"lane": lane_peer(d)}, device_id_type=MESH)
        return _

    def greet_cell(d, _):
        pl.semaphore_signal(barrier, inc=1, device_id={"cell": cell_peer(d)}, device_id_type=MESH)
        return _

    lax.fori_loop(1, LANES, greet_lane, 0)
    hub = me == 0

    @pl.when(hub)
    def _():
        lax.fori_loop(1, cells, greet_cell, 0)


    for fetch in fetches[:3]:
        fetch.wait()
    root = jnp.broadcast_to(jnp.sqrt(power[...]), (LAYERS, W))
    layer = lax.broadcasted_iota(jnp.int32, (LAYERS, W), 0)
    masks = []
    for h in range(2):
        part = slice(h * W, (h + 1) * W)
        picked = jnp.take_along_axis(root, uid[:, part], axis=1, mode="promise_in_bounds")
        granted = layer < lay[:, part]
        masks.append(jnp.where(granted, 1.0, 0.0))
        amplitude = jnp.where(granted, picked, 0.0)
        tx_own[h : h + 1, :] = jnp.sum(amplitude * amplitude, axis=0, keepdims=True) / LAYERS
        spread = swap4([amplitude] * 4)
        for q in range(4):
            amp[4 * h + q] = spread[q]

    def tx_copy(d):
        return pltpu.make_async_remote_copy(
            src_ref=tx_own, dst_ref=tx_all.at[mc], send_sem=ts, recv_sem=tr,
            device_id={"cell": cell_peer(d)}, device_id_type=MESH,
        )

    @pl.when(hub)
    def _():
        pl.semaphore_wait(barrier, LANES - 1 + cells - 1)
        for d in range(1, cells):
            tx_copy(d).start()

    fetches[3].wait()
    for h in range(2):
        part = slice(h * W, (h + 1) * W)
        for ah in range(2):
            for c in range(2):
                turned = swap4([ch[ah * 4 + g, c, :, part] * masks[h] for g in range(4)])
                for q in range(4):
                    sb[2 * (4 * h + q) + ah, c] = turned[q]
    own_amp = amp[me]

    def block_copy(src, dst, send, recv, d):
        return pltpu.make_async_remote_copy(
            src_ref=src.at[pl.ds(2 * lane_peer(d), 2)], dst_ref=dst.at[pl.ds(2 * me, 2)],
            send_sem=send.at[d - 1], recv_sem=recv.at[d - 1],
            device_id={"lane": lane_peer(d)}, device_id_type=MESH,
        )

    def sigma_copy(z):
        return pltpu.make_async_remote_copy(
            src_ref=sig_all.at[z], dst_ref=sig_in, send_sem=ss.at[z - 1], recv_sem=sr,
            device_id={"lane": z}, device_id_type=MESH,
        )

    far_first = (4, 3, 5, 2, 6, 1, 7)
    @pl.when(me != 0)
    def _():
        pl.semaphore_wait(barrier, LANES - 1)

    for d in far_first:
        block_copy(sb, rb, hs, hr, d).start()

    @pl.when(hub)
    def _():
        tx_all[mc] = tx_own[...]
        fetches[4].wait()
        fetches[5].wait()

        arrived = tx_all.at[pl.ds(0, cells - 1)]
        pltpu.make_async_copy(arrived, arrived, tr).wait()
        sigma = jnp.full((2, W), NOISE_FLOOR, F32)
        for k in range(neigh.shape[0]):
            sigma = sigma + coup[k, mc] * tx_all[neigh[k, mc]]
        for h in range(2):
            spread = swap4([sigma[h : h + 1, :]] * 4)
            for q in range(4):
                sig_all[4 * h + q] = spread[q]
        for z in far_first:
            sigma_copy(z).start()
        sig_in[...] = sig_all[0]

    @pl.when(me != 0)
    def _():
        fetches[4].wait()
        fetches[5].wait()

    rb[pl.ds(2 * me, 2)] = sb[pl.ds(2 * me, 2)]
    fetches[6].wait()
    spread_symbols(sym, symf, tmp, sy)

    for d in far_first[::-1]:
        block_copy(sb, rb, hs, hr, d).wait()

    zero = jnp.zeros((8, W), F32)
    for lt in range(2):
        rows = slice(8 * lt, 8 * lt + 8)

        def gram_step(a, acc, rows=rows):
            ar, ai = rb[a, 0, rows, :], rb[a, 1, rows, :]
            out = []
            for m in range(LAYERS):
                br, bi = rb[a, 0, m : m + 1, :], rb[a, 1, m : m + 1, :]
                out.append(acc[2 * m] + (ar * br + ai * bi))
                out.append(acc[2 * m + 1] + (ai * br - ar * bi))
            return tuple(out)

        acc = lax.fori_loop(0, 2 * LANES, gram_step, (zero,) * (2 * LAYERS))
        for m in range(LAYERS):
            ea[0, m, rows, :] = total4(acc[2 * m])
            ea[1, m, rows, :] = total4(acc[2 * m + 1])

    @pl.when(me != 0)
    def _():
        sigma_copy(1).wait_recv()

    @pl.when(hub)
    def _():
        for z in range(1, LANES):
            sigma_copy(z).wait_send()
        arrived = tx_all.at[pl.ds(0, cells - 1)]
        pltpu.make_async_copy(arrived, arrived, ts).wait()

    sigma = sig_in[...]
    diagonal = jnp.zeros((LAYERS, W), F32)
    for m in range(LAYERS):
        diagonal = diagonal + jnp.where(layer == m, ea[0, m] + sigma, 0.0)
    inv_trace = 1.0 / jnp.sum(diagonal, axis=0, keepdims=True)
    for m in range(LAYERS):
        ea[0, m] = jnp.where(layer == m, 1.0 - (ea[0, m] + sigma) * inv_trace, -ea[0, m] * inv_trace)
        ea[1, m] = -ea[1, m] * inv_trace
    column = lanes_of((LAYERS, W)) // 32
    for j in range(4):
        for c in range(2):
            ecol[c, j] = pick4([ea[c, 4 * j + g] for g in range(4)])
        scol[0, j] = ecol[0, j] + jnp.where(layer == 4 * j + column, 1.0, 0.0)
        scol[1, j] = ecol[1, j]

    def products(refs):
        sums = [[[jnp.zeros((LAYERS, W), F32) for j in range(4)] for c in range(2)] for _ in refs]
        for k in range(LAYERS):
            ar, ai = ea[0, k], ea[1, k]
            for out, ref in zip(sums, refs):
                for j in range(4):
                    br, bi = ref[0, j, k : k + 1, :], ref[1, j, k : k + 1, :]
                    out[0][j] = out[0][j] + (ar * br - ai * bi)
                    out[1][j] = out[1][j] + (ar * bi + ai * br)
        return sums

    def put_square(square):
        for c in range(2):
            for j in range(4):
                ecol[c, j] = square[c][j]
                full = spread4(square[c][j])
                for g in range(4):
                    ea[c, 4 * j + g] = full[g]

    put_square(products([ecol])[0])

    def level(i, _):
        square, more = products([ecol, scol])
        for c in range(2):
            for j in range(4):
                scol[c, j] = scol[c, j] + more[c][j]
        put_square(square)
        return _

    lax.fori_loop(1, 5, level, 0)
    (more,) = products([scol])
    for c in range(2):
        for j in range(4):
            full = spread4((scol[c, j] + more[c][j]) * inv_trace)
            for g in range(4):
                ea[c, 4 * j + g] = full[g]

    def apply_step(z, energy):
        sums = [[jnp.zeros((LAYERS, W), F32) for c in range(2)] for ah in range(2)]
        for m in range(LAYERS):
            xr, xi = ea[0, m], ea[1, m]
            for ah in range(2):
                br, bi = rb[2 * z + ah, 0, m : m + 1, :], rb[2 * z + ah, 1, m : m + 1, :]
                sums[ah][0] = sums[ah][0] + (br * xr - bi * xi)
                sums[ah][1] = sums[ah][1] + (br * xi + bi * xr)
        for ah in range(2):
            vr, vi = sums[ah]
            vs[2 * z + ah, 0] = vr
            vs[2 * z + ah, 1] = -vi
            energy = energy + (vr * vr + vi * vi)
        return energy

    energy = total4(lax.fori_loop(0, LANES, apply_step, jnp.zeros((LAYERS, W), F32)))
    scale = own_amp / jnp.sqrt(energy + NORM_EPS)

    def round_step(a, _):
        for c in range(2):
            wsb[a, c] = (vs[a, c] * scale).astype(BF16)
        return _

    lax.fori_loop(0, 2 * LANES, round_step, 0)
    for d in far_first:
        block_copy(wsb, w_out, ws, wr, d).start()
    w_out[pl.ds(2 * me, 2)] = wsb[pl.ds(2 * me, 2)]
    for d in far_first[::-1]:
        block_copy(wsb, w_out, ws, wr, d).wait()

    for h in range(2):
        for ah in range(2):
            for c in range(2):
                turned = swap4([w_out[2 * (4 * h + q) + ah, c].astype(F32) for q in range(4)])
                for g in range(4):
                    wn[h, ah * 4 + g, c] = turned[g]

    for h in range(2):

        def precode(half, _, h=h):
            sums = [[[jnp.zeros((8, W), F32) for i in range(3)] for c in range(2)] for a in range(4)]
            for l in range(LAYERS):
                sr = [sy[h, (2 * l) * 24 + 8 * i : (2 * l) * 24 + 8 * i + 8, :] for i in range(3)]
                si = [sy[h, (2 * l + 1) * 24 + 8 * i : (2 * l + 1) * 24 + 8 * i + 8, :] for i in range(3)]
                for a in range(4):
                    wr = wn[h, 4 * half + a, 0, l : l + 1, :]
                    wi = wn[h, 4 * half + a, 1, l : l + 1, :]
                    for i in range(3):
                        sums[a][0][i] = sums[a][0][i] + (wr * sr[i] - wi * si[i])
                        sums[a][1][i] = sums[a][1][i] + (wr * si[i] + wi * sr[i])
            for a in range(4):
                for c in range(2):
                    for i in range(3):
                        gf[c, h, pl.ds(64 * i + 4 * half + a, 8, stride=8), :] = sums[a][c][i]
            return _

        lax.fori_loop(0, 2, precode, 0)

    for c in range(2):
        for h in range(2):
            value = gf[c, h]
            high = value.astype(BF16)
            cols = slice(c * PRBS + h * W, c * PRBS + (h + 1) * W)
            lhs[:, cols] = high

    fetches[7].wait()
    fetches[8].wait()

    def section(nt, _):
        result = jnp.dot(lhs[...], dft[nt], preferred_element_type=F32)
        for s in range(SYMS):
            part = [[None, None] for _ in range(4)]
            for k in range(SUBC):
                row = (s * SUBC + k) * 8
                tr, ti = result[row : row + 8, 0:W], result[row : row + 8, W : 2 * W]
                cr, ci = twist[nt, k : k + 1, :], twist[nt, SUBC + k : SUBC + k + 1, :]
                ur, ui = tr * cr - ti * ci, tr * ci + ti * cr
                held = part[k % 4]
                held[0] = ur if held[0] is None else held[0] + ur
                held[1] = ui if held[1] is None else held[1] + ui
            (ar, ai), (br, bi), (cr, ci), (dr, di) = part
            pr, pi, mr, mi = ar + cr, ai + ci, ar - cr, ai - ci
            qr, qi, nr, ni = br + dr, bi + di, br - dr, bi - di
            outs = ((pr + qr, pi + qi), (mr - ni, mi + nr), (pr - qr, pi - qi), (mr + ni, mi - nr))
            for n2 in range(4):
                for c in range(2):
                    out[pl.ds(c * 64 + (n2 * 8 + nt) * 2 + s, 8, stride=128), :] = outs[n2][c]
        return _

    lax.fori_loop(0, 8, section, 0)


def ofdm_tables():
    p = np.arange(PRBS)[:, None]
    n = np.arange(1024)[None, :]
    angle = 2.0 * math.pi * ((3 * p * n) % 1024) / 1024
    cos, sin = np.cos(angle), np.sin(angle)
    real = np.concatenate([cos, -sin], 0).reshape(2 * PRBS, 8, 1, W)
    imag = np.concatenate([sin, cos], 0).reshape(2 * PRBS, 8, 1, W)
    dft = np.concatenate([real, imag], 2).reshape(2 * PRBS, 8, 2 * W).transpose(1, 0, 2)
    k = np.arange(SUBC)[:, None]
    angle = 2.0 * math.pi * (((k - 1536) * n) % NFFT) / NFFT
    twist = np.concatenate([np.cos(angle), np.sin(angle)], 0) / math.sqrt(NFFT)
    twist = twist.reshape(2 * SUBC, 8, W).transpose(1, 0, 2)
    return jnp.asarray(dft, BF16), jnp.asarray(twist, F32)


def slot(cells, channel, symbols, layers, user_ids, user_power, neighbours, coupling):
    dft, twist = ofdm_tables()
    args = (channel, symbols, layers, user_ids, user_power, neighbours, coupling, dft, twist)
    block = (2 * LANES, 2, LAYERS, W)
    dma = pltpu.SemaphoreType.DMA
    held = [(pltpu.SMEM if i in (5, 6) else pltpu.VMEM)(x.shape, x.dtype) for i, x in enumerate(args)]
    return pl.pallas_call(
        functools.partial(slot_kernel, cells),
        out_shape=pltpu.VMEM((1024, W), F32),
        in_specs=[pl.BlockSpec(memory_space=pl.ANY)] * len(args),
        out_specs=pl.BlockSpec(memory_space=pltpu.VMEM),
        scratch_shapes=held + [
            pltpu.VMEM(block, F32),
            pltpu.VMEM(block, F32),
            pltpu.VMEM((LANES, LAYERS, W), F32),
            pltpu.VMEM((2, W), F32),
            pltpu.VMEM((cells, 2, W), F32),
            pltpu.VMEM((LANES, 1, W), F32),
            pltpu.VMEM((1, W), F32),
            pltpu.VMEM((2, LAYERS, LAYERS, W), F32),
            pltpu.VMEM((2, 4, LAYERS, W), F32),
            pltpu.VMEM((2, 4, LAYERS, W), F32),
            pltpu.VMEM(block, F32),
            pltpu.VMEM(block, BF16),
            pltpu.VMEM(block, BF16),
            pltpu.VMEM((64, 3072), F32),
            pltpu.VMEM((8, 64, 384), F32),
            pltpu.VMEM((2, 768, W), F32),
            pltpu.VMEM((2, 8, 2, LAYERS, W), F32),
            pltpu.VMEM((2, 2, 192, W), F32),
            pltpu.VMEM((192, 512), BF16),
            dma((len(args),)),
            dma((LANES - 1,)),
            dma((LANES - 1,)),
            dma,
            dma,
            dma((LANES - 1,)),
            dma,
            dma((LANES - 1,)),
            dma((LANES - 1,)),
        ],
        compiler_params=pltpu.CompilerParams(collective_id=0, has_side_effects=True),
        name="slot",
    )(*args)


def per_device(cells, channel, symbols, layers, user_ids, user_power, neighbours, coupling):
    samples = slot(
        cells, channel[0], symbols[0].reshape(2 * LAYERS, SYMS, 3072), layers, user_ids[0], user_power,
        neighbours.T, coupling.T,
    )
    samples = samples.reshape(8, 2, 32, SYMS, W).transpose(0, 1, 3, 2, 4)
    return samples.reshape(1, 8, 2, SYMS, NFFT)


def solution(mesh):
    in_specs = (
        P("cell", "lane", None, None, None),
        P("cell", None, None, None, None),
        P("cell", None),
        P("cell", None, None),
        P("cell", None),
        P(),
        P(),
    )
    out_specs = P("cell", "lane", None, None, None)
    return jax.shard_map(
        functools.partial(per_device, mesh.shape["cell"]),
        mesh=mesh, in_specs=in_specs, out_specs=out_specs, check_vma=False,
    )
```

```python
import functools
import math

import jax
import jax.numpy as jnp
import numpy as np
from jax import lax
from jax.experimental import pallas as pl
from jax.experimental.pallas import tpu as pltpu
from jax.sharding import PartitionSpec as P

MESH = pl.DeviceIdType.MESH
NFFT = 4096
PRBS = 256
SUBC = 12
SYMS = 2
LAYERS = 16
NORM_EPS = 1e-06
NOISE_FLOOR = 0.05
LANES = 8
W = 128
F32 = jnp.float32
BF16 = jnp.bfloat16


def lanes_of(shape):
    return lax.broadcasted_iota(jnp.int32, shape, len(shape) - 1)


def swap4(x):
    lane = lanes_of(x[0].shape)
    low_half = lane < 64
    even = lax.rem(lane, 64) < 32
    y0 = jnp.where(low_half, x[0], pltpu.roll(x[2], 64, 1))
    y2 = jnp.where(low_half, pltpu.roll(x[0], 64, 1), x[2])
    y1 = jnp.where(low_half, x[1], pltpu.roll(x[3], 64, 1))
    y3 = jnp.where(low_half, pltpu.roll(x[1], 64, 1), x[3])
    z0 = jnp.where(even, y0, pltpu.roll(y1, 32, 1))
    z1 = jnp.where(even, pltpu.roll(y0, 96, 1), y1)
    z2 = jnp.where(even, y2, pltpu.roll(y3, 32, 1))
    z3 = jnp.where(even, pltpu.roll(y2, 96, 1), y3)
    return [z0, z1, z2, z3]


def pick4(x):
    lane = lanes_of(x[0].shape)
    return jnp.where(
        lane < 64,
        jnp.where(lane < 32, x[0], x[1]),
        jnp.where(lane < 96, x[2], x[3]),
    )


def spread4(x):
    r = [x, pltpu.roll(x, 32, 1), pltpu.roll(x, 64, 1), pltpu.roll(x, 96, 1)]
    return [pick4([r[(h - g) % 4] for h in range(4)]) for g in range(4)]


def total4(x):
    x = x + pltpu.roll(x, 64, 1)
    return x + pltpu.roll(x, 32, 1)


def spread_symbols(sym, symf, tmp, sy):
    def widen(lc, _):
        pair = sym[lc].astype(F32)
        symf[pl.ds(lc, 1), :] = pair[0:1, :]
        symf[pl.ds(2 * LAYERS + lc, 1), :] = pair[1:2, :]
        return _

    lax.fori_loop(0, 2 * LAYERS, widen, 0)
    j = lax.broadcasted_iota(jnp.int32, (384, 384), 0)
    o = lax.broadcasted_iota(jnp.int32, (384, 384), 1)
    source = SUBC * lax.rem(o, 32) + o // 32
    order = jnp.where(j == source, 1.0, 0.0).astype(BF16)
    for z in range(8):
        tmp[z] = jnp.dot(symf[:, 384 * z : 384 * (z + 1)].astype(BF16), order, preferred_element_type=F32)
    for h in range(2):
        for t in range(3):
            turned = swap4([tmp[4 * h + q, :, W * t : W * (t + 1)] for q in range(4)])
            for kk in range(4):
                k = 4 * t + kk
                for s in range(SYMS):
                    for b in range(4):
                        sy[h, pl.ds(b * 8 * 24 + s * SUBC + k, 8, stride=24), :] = turned[kk][
                            s * 32 + b * 8 : s * 32 + b * 8 + 8, :
                        ]


GROUP = 8
PACK_ROWS = 6


def group_total(x):
    position = lax.rem(lanes_of(x.shape), GROUP)
    for step in (1, 2, 4):
        upper = lax.rem(position // step, 2) == 1
        x = x + jnp.where(upper, pltpu.roll(x, step, 1), pltpu.roll(x, W - step, 1))
    return x


def pack_tables(count):
    shape = (LAYERS, W)
    layer = lax.broadcasted_iota(jnp.int32, shape, 0)
    lane = lanes_of(shape)
    position = lax.rem(lane, GROUP)
    base = lane - position
    granted = layer < count
    one = jnp.where(granted, 1, 0)
    rank = one
    for step in (1, 2, 4):
        rank = rank + jnp.where(position >= step, pltpu.roll(rank, step, 1), 0)
    rank = rank - one
    number = group_total(one)
    offset = group_total(jnp.minimum(count, layer))
    target = lax.rem(offset + rank, GROUP)
    unpack_lane = base + target
    turn = lax.rem(position - offset + LAYERS * GROUP, GROUP)
    unpack_row = jnp.minimum((offset + turn) // GROUP, PACK_ROWS - 1)
    marked = jnp.where(granted, target, GROUP)
    pack_lane = lane
    for step in range(GROUP):
        if step == 0:
            seen = marked
        else:
            seen = jnp.where(
                position + step < GROUP, pltpu.roll(marked, W - step, 1), pltpu.roll(marked, GROUP - step, 1)
            )
        source = base + lax.rem(position + step, GROUP)
        pack_lane = jnp.where(seen == position, source, pack_lane)
    row = lax.broadcasted_iota(jnp.int32, (8, W), 0)
    pack_layer = jnp.zeros((8, W), jnp.int32)
    for r in range(PACK_ROWS):
        passed = jnp.where(offset + number <= GROUP * r + position, 1, 0)
        level = jnp.minimum(jnp.sum(passed, axis=0, keepdims=True), LAYERS - 1)
        pack_layer = jnp.where(row == r, level, pack_layer)
    return granted, pack_lane, pack_layer, unpack_row, unpack_lane


def along(x, index, axis):
    return jnp.take_along_axis(x, index, axis=axis, mode="promise_in_bounds")


def pack(x, tables):
    pack_lane, pack_layer = tables[1], tables[2]
    turned = [along(x[8 * i : 8 * i + 8], pack_lane[8 * i : 8 * i + 8], 1) for i in range(2)]
    within = lax.rem(pack_layer, 8)
    return jnp.where(pack_layer < 8, along(turned[0], within, 0), along(turned[1], within, 0))


def unpack(x, tables, first=0):
    granted, unpack_row, unpack_lane = tables[0], tables[3] + first, tables[4]
    parts = []
    for i in range(2):
        rows = slice(8 * i, 8 * i + 8)
        parts.append(along(along(x, unpack_row[rows], 0), unpack_lane[rows], 1))
    return jnp.where(granted, jnp.concatenate(parts, axis=0), 0.0)


def packed_start(i):
    return min(PACK_ROWS * i, 4 * PACK_ROWS - 8)


def slot_kernel(
    cells, ch_any, sym_any, lay_any, uid_any, power_any, neigh_any, coup_any, dft_any, twist_any, out,
    ch, sym, lay, uid, power, neigh, coup, dft, twist,
    sb, rb, hb, amp, lay_all, wsf, wrf, tx_own, tx_all, sig_all, sig_in, ea, ecol, scol, vs, wsb, w_out,
    symf, tmp, sy, wn, gf, lhs,
    ins, hs, hr, ts, tr, ss, sr, ws, wr, ready,
):
    fetches = [
        pltpu.make_async_copy(source, held, ins.at[i])
        for i, (source, held) in enumerate((
            (lay_any, lay), (uid_any, uid), (power_any, power), (ch_any, ch), (neigh_any, neigh),
            (coup_any, coup), (sym_any, sym), (dft_any, dft), (twist_any, twist),
        ))
    ]
    for fetch in fetches:
        fetch.start()
    me = lax.axis_index("lane")
    mc = lax.axis_index("cell")
    barrier = pltpu.get_barrier_semaphore()

    def lane_peer(d):
        return lax.rem(me + d, LANES)

    def cell_peer(d):
        return lax.rem(mc + d, cells)

    hub = me == 0

    def greet_lane(d, carry):
        peer = lane_peer(d)

        @pl.when(peer != 0)
        def _():
            pl.semaphore_signal(barrier, inc=1, device_id={"lane": peer}, device_id_type=MESH)

        return carry

    def greet_cell(d, _):
        pl.semaphore_signal(barrier, inc=1, device_id={"cell": cell_peer(d)}, device_id_type=MESH)
        return _

    lax.fori_loop(1, LANES, greet_lane, 0)
    @pl.when(hub)
    def _():
        lax.fori_loop(1, cells, greet_cell, 0)


    for fetch in fetches[:3]:
        fetch.wait()
    root = jnp.broadcast_to(jnp.sqrt(power[...]), (LAYERS, W))
    layer = lax.broadcasted_iota(jnp.int32, (LAYERS, W), 0)
    for h in range(2):
        part = slice(h * W, (h + 1) * W)
        picked = jnp.take_along_axis(root, uid[:, part], axis=1, mode="promise_in_bounds")
        granted = layer < lay[:, part]
        spread = swap4([lay[:, part]] * 4)
        for q in range(4):
            lay_all[4 * h + q] = spread[q]
        amplitude = jnp.where(granted, picked, 0.0)
        tx_own[h : h + 1, :] = jnp.sum(amplitude * amplitude, axis=0, keepdims=True) / LAYERS
        spread = swap4([amplitude] * 4)
        for q in range(4):
            amp[4 * h + q] = spread[q]

    def tx_copy(d):
        return pltpu.make_async_remote_copy(
            src_ref=tx_own, dst_ref=tx_all.at[mc], send_sem=ts, recv_sem=tr,
            device_id={"cell": cell_peer(d)}, device_id_type=MESH,
        )

    @pl.when(hub)
    def _():
        pl.semaphore_wait(barrier, cells - 1)
        for d in range(1, cells):
            tx_copy(d).start()

    natural = [pack_tables(lay[:, h * W : (h + 1) * W]) for h in range(2)]
    fetches[3].wait()
    for h in range(2):
        part = slice(h * W, (h + 1) * W)
        for ah in range(2):
            for c in range(2):
                turned = swap4([pack(ch[ah * 4 + g, c, :, part], natural[h]) for g in range(4)])
                first = PACK_ROWS * (2 * ah + c)
                for q in range(4):
                    sb[4 * h + q, first : first + PACK_ROWS, :] = turned[q][:PACK_ROWS]
    own_amp = amp[me]

    def block_copy(src, dst, send, recv, d):
        return pltpu.make_async_remote_copy(
            src_ref=src.at[lane_peer(d)], dst_ref=dst.at[me],
            send_sem=send.at[d - 1], recv_sem=recv.at[d - 1],
            device_id={"lane": lane_peer(d)}, device_id_type=MESH,
        )

    def sigma_copy(z):
        return pltpu.make_async_remote_copy(
            src_ref=sig_all.at[z], dst_ref=sig_in, send_sem=ss.at[z - 1], recv_sem=sr,
            device_id={"lane": z}, device_id_type=MESH,
        )

    far_first = (4, 3, 5, 2, 6, 1, 7)
    @pl.when(hub)
    def _():
        pl.semaphore_wait(ready, LANES - 1)

    @pl.when(me != 0)
    def _():
        pl.semaphore_wait(barrier, LANES - 1)

        pl.semaphore_signal(ready, inc=1, device_id={"lane": 0}, device_id_type=MESH)

    for d in far_first:
        block_copy(sb, rb, hs, hr, d).start()

    @pl.when(hub)
    def _():
        tx_all[mc] = tx_own[...]
        fetches[4].wait()
        fetches[5].wait()

        arrived = tx_all.at[pl.ds(0, cells - 1)]
        pltpu.make_async_copy(arrived, arrived, tr).wait()
        sigma = jnp.full((2, W), NOISE_FLOOR, F32)
        for k in range(neigh.shape[0]):
            sigma = sigma + coup[k, mc] * tx_all[neigh[k, mc]]
        for h in range(2):
            spread = swap4([sigma[h : h + 1, :]] * 4)
            for q in range(4):
                sig_all[4 * h + q] = spread[q]
        for z in far_first:
            sigma_copy(z).start()
        sig_in[...] = sig_all[0]

    @pl.when(me != 0)
    def _():
        fetches[4].wait()
        fetches[5].wait()

    own_tables = pack_tables(lay_all[me])

    def unpack_block(source, z):
        for ah in range(2):
            for c in range(2):
                i = 2 * ah + c
                first = packed_start(i)
                hb[2 * z + ah, c] = unpack(
                    source[z, first : first + 8, :], own_tables, PACK_ROWS * i - first
                )

    unpack_block(sb, me)
    fetches[6].wait()
    spread_symbols(sym, symf, tmp, sy)

    for d in far_first[::-1]:
        block_copy(sb, rb, hs, hr, d).wait()
        unpack_block(rb, lax.rem(me - d + LANES, LANES))

    zero = jnp.zeros((8, W), F32)
    for lt in range(2):
        rows = slice(8 * lt, 8 * lt + 8)

        def gram_step(a, acc, rows=rows):
            ar, ai = hb[a, 0, rows, :], hb[a, 1, rows, :]
            out = []
            for m in range(LAYERS):
                br, bi = hb[a, 0, m : m + 1, :], hb[a, 1, m : m + 1, :]
                out.append(acc[2 * m] + (ar * br + ai * bi))
                out.append(acc[2 * m + 1] + (ai * br - ar * bi))
            return tuple(out)

        acc = lax.fori_loop(0, 2 * LANES, gram_step, (zero,) * (2 * LAYERS))
        for m in range(LAYERS):
            ea[0, m, rows, :] = total4(acc[2 * m])
            ea[1, m, rows, :] = total4(acc[2 * m + 1])

    @pl.when(me != 0)
    def _():
        sigma_copy(1).wait_recv()

    @pl.when(hub)
    def _():
        for z in range(1, LANES):
            sigma_copy(z).wait_send()
        arrived = tx_all.at[pl.ds(0, cells - 1)]
        pltpu.make_async_copy(arrived, arrived, ts).wait()

    sigma = sig_in[...]
    diagonal = jnp.zeros((LAYERS, W), F32)
    for m in range(LAYERS):
        diagonal = diagonal + jnp.where(layer == m, ea[0, m] + sigma, 0.0)
    inv_trace = 1.0 / jnp.sum(diagonal, axis=0, keepdims=True)
    for m in range(LAYERS):
        ea[0, m] = jnp.where(layer == m, 1.0 - (ea[0, m] + sigma) * inv_trace, -ea[0, m] * inv_trace)
        ea[1, m] = -ea[1, m] * inv_trace
    column = lanes_of((LAYERS, W)) // 32
    for j in range(4):
        for c in range(2):
            ecol[c, j] = pick4([ea[c, 4 * j + g] for g in range(4)])
        scol[0, j] = ecol[0, j] + jnp.where(layer == 4 * j + column, 1.0, 0.0)
        scol[1, j] = ecol[1, j]

    def products(refs):
        sums = [[[jnp.zeros((LAYERS, W), F32) for j in range(4)] for c in range(2)] for _ in refs]
        for k in range(LAYERS):
            ar, ai = ea[0, k], ea[1, k]
            for out, ref in zip(sums, refs):
                for j in range(4):
                    br, bi = ref[0, j, k : k + 1, :], ref[1, j, k : k + 1, :]
                    out[0][j] = out[0][j] + (ar * br - ai * bi)
                    out[1][j] = out[1][j] + (ar * bi + ai * br)
        return sums

    def put_square(square):
        for c in range(2):
            for j in range(4):
                ecol[c, j] = square[c][j]
                full = spread4(square[c][j])
                for g in range(4):
                    ea[c, 4 * j + g] = full[g]

    put_square(products([ecol])[0])

    def level(i, _):
        square, more = products([ecol, scol])
        for c in range(2):
            for j in range(4):
                scol[c, j] = scol[c, j] + more[c][j]
        put_square(square)
        return _

    lax.fori_loop(1, 5, level, 0)
    (more,) = products([scol])
    for c in range(2):
        for j in range(4):
            full = spread4((scol[c, j] + more[c][j]) * inv_trace)
            for g in range(4):
                ea[c, 4 * j + g] = full[g]

    def apply_step(z, energy):
        sums = [[jnp.zeros((LAYERS, W), F32) for c in range(2)] for ah in range(2)]
        for m in range(LAYERS):
            xr, xi = ea[0, m], ea[1, m]
            for ah in range(2):
                br, bi = hb[2 * z + ah, 0, m : m + 1, :], hb[2 * z + ah, 1, m : m + 1, :]
                sums[ah][0] = sums[ah][0] + (br * xr - bi * xi)
                sums[ah][1] = sums[ah][1] + (br * xi + bi * xr)
        for ah in range(2):
            vr, vi = sums[ah]
            vs[2 * z + ah, 0] = vr
            vs[2 * z + ah, 1] = -vi
            energy = energy + (vr * vr + vi * vi)
        return energy

    energy = total4(lax.fori_loop(0, LANES, apply_step, jnp.zeros((LAYERS, W), F32)))
    scale = own_amp / jnp.sqrt(energy + NORM_EPS)

    def round_block(z, target):
        for ah in range(2):
            for c in range(2):
                first = PACK_ROWS * (2 * ah + c)
                wsf[z, first : first + PACK_ROWS, :] = pack(vs[2 * z + ah, c] * scale, own_tables)[:PACK_ROWS]
        target[z] = wsf[z].astype(BF16)

    for d in far_first:
        round_block(lane_peer(d), wsb)
        block_copy(wsb, w_out, ws, wr, d).start()
    round_block(me, w_out)
    natural = [pack_tables(lay[:, h * W : (h + 1) * W]) for h in range(2)]
    for d in far_first[::-1]:
        block_copy(wsb, w_out, ws, wr, d).wait()
    for z in range(LANES):
        wrf[z] = w_out[z].astype(F32)

    for h in range(2):
        for ah in range(2):
            for c in range(2):
                i = 2 * ah + c
                first = packed_start(i)
                turned = swap4([wrf[4 * h + q, first : first + 8, :] for q in range(4)])
                for g in range(4):
                    wn[h, ah * 4 + g, c] = unpack(turned[g], natural[h], PACK_ROWS * i - first)

    for h in range(2):

        def precode(half, _, h=h):
            sums = [[[jnp.zeros((8, W), F32) for i in range(3)] for c in range(2)] for a in range(4)]
            for l in range(LAYERS):
                sr = [sy[h, (2 * l) * 24 + 8 * i : (2 * l) * 24 + 8 * i + 8, :] for i in range(3)]
                si = [sy[h, (2 * l + 1) * 24 + 8 * i : (2 * l + 1) * 24 + 8 * i + 8, :] for i in range(3)]
                for a in range(4):
                    wr = wn[h, 4 * half + a, 0, l : l + 1, :]
                    wi = wn[h, 4 * half + a, 1, l : l + 1, :]
                    for i in range(3):
                        sums[a][0][i] = sums[a][0][i] + (wr * sr[i] - wi * si[i])
                        sums[a][1][i] = sums[a][1][i] + (wr * si[i] + wi * sr[i])
            for a in range(4):
                for c in range(2):
                    for i in range(3):
                        gf[c, h, pl.ds(64 * i + 4 * half + a, 8, stride=8), :] = sums[a][c][i]
            return _

        lax.fori_loop(0, 2, precode, 0)

    for c in range(2):
        for h in range(2):
            value = gf[c, h]
            high = value.astype(BF16)
            cols = slice(c * PRBS + h * W, c * PRBS + (h + 1) * W)
            lhs[:, cols] = high

    fetches[7].wait()
    fetches[8].wait()

    def section(nt, _):
        result = jnp.dot(lhs[...], dft[nt], preferred_element_type=F32)
        for s in range(SYMS):
            part = [[None, None] for _ in range(4)]
            for k in range(SUBC):
                row = (s * SUBC + k) * 8
                tr, ti = result[row : row + 8, 0:W], result[row : row + 8, W : 2 * W]
                cr, ci = twist[nt, k : k + 1, :], twist[nt, SUBC + k : SUBC + k + 1, :]
                ur, ui = tr * cr - ti * ci, tr * ci + ti * cr
                held = part[k % 4]
                held[0] = ur if held[0] is None else held[0] + ur
                held[1] = ui if held[1] is None else held[1] + ui
            (ar, ai), (br, bi), (cr, ci), (dr, di) = part
            pr, pi, mr, mi = ar + cr, ai + ci, ar - cr, ai - ci
            qr, qi, nr, ni = br + dr, bi + di, br - dr, bi - di
            outs = ((pr + qr, pi + qi), (mr - ni, mi + nr), (pr - qr, pi - qi), (mr + ni, mi - nr))
            for n2 in range(4):
                for c in range(2):
                    out[pl.ds(c * 64 + (n2 * 8 + nt) * 2 + s, 8, stride=128), :] = outs[n2][c]
        return _

    lax.fori_loop(0, 8, section, 0)


def ofdm_tables():
    p = np.arange(PRBS)[:, None]
    n = np.arange(1024)[None, :]
    angle = 2.0 * math.pi * ((3 * p * n) % 1024) / 1024
    cos, sin = np.cos(angle), np.sin(angle)
    real = np.concatenate([cos, -sin], 0).reshape(2 * PRBS, 8, 1, W)
    imag = np.concatenate([sin, cos], 0).reshape(2 * PRBS, 8, 1, W)
    dft = np.concatenate([real, imag], 2).reshape(2 * PRBS, 8, 2 * W).transpose(1, 0, 2)
    k = np.arange(SUBC)[:, None]
    angle = 2.0 * math.pi * (((k - 1536) * n) % NFFT) / NFFT
    twist = np.concatenate([np.cos(angle), np.sin(angle)], 0) / math.sqrt(NFFT)
    twist = twist.reshape(2 * SUBC, 8, W).transpose(1, 0, 2)
    return jnp.asarray(dft, BF16), jnp.asarray(twist, F32)


def slot(cells, channel, symbols, layers, user_ids, user_power, neighbours, coupling):
    dft, twist = ofdm_tables()
    args = (channel, symbols, layers, user_ids, user_power, neighbours, coupling, dft, twist)
    block = (2 * LANES, 2, LAYERS, W)
    packed = (LANES, 4 * PACK_ROWS, W)
    dma = pltpu.SemaphoreType.DMA
    held = [(pltpu.SMEM if i in (5, 6) else pltpu.VMEM)(x.shape, x.dtype) for i, x in enumerate(args)]
    return pl.pallas_call(
        functools.partial(slot_kernel, cells),
        out_shape=pltpu.VMEM((1024, W), F32),
        in_specs=[pl.BlockSpec(memory_space=pl.ANY)] * len(args),
        out_specs=pl.BlockSpec(memory_space=pltpu.VMEM),
        scratch_shapes=held + [
            pltpu.VMEM(packed, F32),
            pltpu.VMEM(packed, F32),
            pltpu.VMEM(block, F32),
            pltpu.VMEM((LANES, LAYERS, W), F32),
            pltpu.VMEM((LANES, 1, W), jnp.int32),
            pltpu.VMEM(packed, F32),
            pltpu.VMEM(packed, F32),
            pltpu.VMEM((2, W), F32),
            pltpu.VMEM((cells, 2, W), F32),
            pltpu.VMEM((LANES, 1, W), F32),
            pltpu.VMEM((1, W), F32),
            pltpu.VMEM((2, LAYERS, LAYERS, W), F32),
            pltpu.VMEM((2, 4, LAYERS, W), F32),
            pltpu.VMEM((2, 4, LAYERS, W), F32),
            pltpu.VMEM(block, F32),
            pltpu.VMEM(packed, BF16),
            pltpu.VMEM(packed, BF16),
            pltpu.VMEM((64, 3072), F32),
            pltpu.VMEM((8, 64, 384), F32),
            pltpu.VMEM((2, 768, W), F32),
            pltpu.VMEM((2, 8, 2, LAYERS, W), F32),
            pltpu.VMEM((2, 2, 192, W), F32),
            pltpu.VMEM((192, 512), BF16),
            dma((len(args),)),
            dma((LANES - 1,)),
            dma((LANES - 1,)),
            dma,
            dma,
            dma((LANES - 1,)),
            dma,
            dma((LANES - 1,)),
            dma((LANES - 1,)),
            pltpu.SemaphoreType.REGULAR,
        ],
        compiler_params=pltpu.CompilerParams(collective_id=0, has_side_effects=True),
        name="slot",
    )(*args)


def per_device(cells, channel, symbols, layers, user_ids, user_power, neighbours, coupling):
    samples = slot(
        cells, channel[0], symbols[0].reshape(2 * LAYERS, SYMS, 3072), layers, user_ids[0], user_power,
        neighbours.T, coupling.T,
    )
    samples = samples.reshape(8, 2, 32, SYMS, W).transpose(0, 1, 3, 2, 4)
    return samples.reshape(1, 8, 2, SYMS, NFFT)


def solution(mesh):
    in_specs = (
        P("cell", "lane", None, None, None),
        P("cell", None, None, None, None),
        P("cell", None),
        P("cell", None, None),
        P("cell", None),
        P(),
        P(),
    )
    out_specs = P("cell", "lane", None, None, None)
    return jax.shard_map(
        functools.partial(per_device, mesh.shape["cell"]),
        mesh=mesh, in_specs=in_specs, out_specs=out_specs, check_vma=False,
    )
```

```python
import functools
import math

import jax
import jax.numpy as jnp
import numpy as np
from jax import lax
from jax.experimental import pallas as pl
from jax.experimental.pallas import tpu as pltpu
from jax.sharding import PartitionSpec as P

MESH = pl.DeviceIdType.MESH
NFFT = 4096
PRBS = 256
SUBC = 12
SYMS = 2
LAYERS = 16
NORM_EPS = 1e-06
NOISE_FLOOR = 0.05
LANES = 8
W = 128
F32 = jnp.float32
BF16 = jnp.bfloat16


def lanes_of(shape):
    return lax.broadcasted_iota(jnp.int32, shape, len(shape) - 1)


def swap4(x):
    lane = lanes_of(x[0].shape)
    low_half = lane < 64
    even = lax.rem(lane, 64) < 32
    y0 = jnp.where(low_half, x[0], pltpu.roll(x[2], 64, 1))
    y2 = jnp.where(low_half, pltpu.roll(x[0], 64, 1), x[2])
    y1 = jnp.where(low_half, x[1], pltpu.roll(x[3], 64, 1))
    y3 = jnp.where(low_half, pltpu.roll(x[1], 64, 1), x[3])
    z0 = jnp.where(even, y0, pltpu.roll(y1, 32, 1))
    z1 = jnp.where(even, pltpu.roll(y0, 96, 1), y1)
    z2 = jnp.where(even, y2, pltpu.roll(y3, 32, 1))
    z3 = jnp.where(even, pltpu.roll(y2, 96, 1), y3)
    return [z0, z1, z2, z3]


def pick4(x):
    lane = lanes_of(x[0].shape)
    return jnp.where(
        lane < 64,
        jnp.where(lane < 32, x[0], x[1]),
        jnp.where(lane < 96, x[2], x[3]),
    )


def spread4(x):
    r = [x, pltpu.roll(x, 32, 1), pltpu.roll(x, 64, 1), pltpu.roll(x, 96, 1)]
    return [pick4([r[(h - g) % 4] for h in range(4)]) for g in range(4)]


def total4(x):
    x = x + pltpu.roll(x, 64, 1)
    return x + pltpu.roll(x, 32, 1)


def spread_symbols(sym, symf, tmp, sy):
    def widen(lc, _):
        pair = sym[lc].astype(F32)
        row = lax.rem(lc, 2) * LAYERS + lc // 2
        symf[pl.ds(row, 1), :] = pair[0:1, :]
        symf[pl.ds(2 * LAYERS + row, 1), :] = pair[1:2, :]
        return _

    lax.fori_loop(0, 2 * LAYERS, widen, 0)
    j = lax.broadcasted_iota(jnp.int32, (384, 384), 0)
    o = lax.broadcasted_iota(jnp.int32, (384, 384), 1)
    source = SUBC * lax.rem(o, 32) + o // 32
    order = jnp.where(j == source, 1.0, 0.0).astype(BF16)
    for z in range(8):
        tmp[z] = jnp.dot(symf[:, 384 * z : 384 * (z + 1)].astype(BF16), order, preferred_element_type=F32)
    for h in range(2):
        for t in range(3):
            turned = swap4([tmp[4 * h + q, :, W * t : W * (t + 1)] for q in range(4)])
            for kk in range(4):
                k = 4 * t + kk
                for s in range(SYMS):
                    parts = [turned[kk][s * 32 + b * 8 : s * 32 + b * 8 + 8, :] for b in range(4)]
                    parts += [parts[0] + parts[2], parts[1] + parts[3]]
                    for b, part in enumerate(parts):
                        sy[h, pl.ds(b * 8 * 24 + s * SUBC + k, 8, stride=24), :] = part


GROUP = 8
PACK_ROWS = 6


def group_total(x):
    position = lax.rem(lanes_of(x.shape), GROUP)
    for step in (1, 2, 4):
        upper = lax.rem(position // step, 2) == 1
        x = x + jnp.where(upper, pltpu.roll(x, step, 1), pltpu.roll(x, W - step, 1))
    return x


def pack_tables(count):
    shape = (LAYERS, W)
    layer = lax.broadcasted_iota(jnp.int32, shape, 0)
    lane = lanes_of(shape)
    position = lax.rem(lane, GROUP)
    base = lane - position
    granted = layer < count
    one = jnp.where(granted, 1, 0)
    rank = one
    for step in (1, 2, 4):
        rank = rank + jnp.where(position >= step, pltpu.roll(rank, step, 1), 0)
    rank = rank - one
    number = group_total(one)
    offset = group_total(jnp.minimum(count, layer))
    target = lax.rem(offset + rank, GROUP)
    unpack_lane = base + target
    turn = lax.rem(position - offset + LAYERS * GROUP, GROUP)
    unpack_row = jnp.minimum((offset + turn) // GROUP, PACK_ROWS - 1)
    marked = jnp.where(granted, target, GROUP)
    pack_lane = lane
    for step in range(GROUP):
        if step == 0:
            seen = marked
        else:
            seen = jnp.where(
                position + step < GROUP, pltpu.roll(marked, W - step, 1), pltpu.roll(marked, GROUP - step, 1)
            )
        source = base + lax.rem(position + step, GROUP)
        pack_lane = jnp.where(seen == position, source, pack_lane)
    row = lax.broadcasted_iota(jnp.int32, (8, W), 0)
    pack_layer = jnp.zeros((8, W), jnp.int32)
    for r in range(PACK_ROWS):
        passed = jnp.where(offset + number <= GROUP * r + position, 1, 0)
        level = jnp.minimum(jnp.sum(passed, axis=0, keepdims=True), LAYERS - 1)
        pack_layer = jnp.where(row == r, level, pack_layer)
    return granted, pack_lane, pack_layer, unpack_row, unpack_lane


def along(x, index, axis):
    return jnp.take_along_axis(x, index, axis=axis, mode="promise_in_bounds")


def pack(x, tables):
    pack_lane, pack_layer = tables[1], tables[2]
    turned = [along(x[8 * i : 8 * i + 8], pack_lane[8 * i : 8 * i + 8], 1) for i in range(2)]
    within = lax.rem(pack_layer, 8)
    return jnp.where(pack_layer < 8, along(turned[0], within, 0), along(turned[1], within, 0))


def unpack(x, tables, first=0):
    granted, unpack_row, unpack_lane = tables[0], tables[3] + first, tables[4]
    parts = []
    for i in range(2):
        rows = slice(8 * i, 8 * i + 8)
        parts.append(along(along(x, unpack_row[rows], 0), unpack_lane[rows], 1))
    return jnp.where(granted, jnp.concatenate(parts, axis=0), 0.0)


def packed_start(i):
    return min(PACK_ROWS * i, 4 * PACK_ROWS - 8)


def slot_kernel(
    cells, ch_any, sym_any, lay_any, uid_any, power_any, neigh_any, coup_any, dft_any, twist_any, out,
    ch, sym, lay, uid, power, neigh, coup, dft, twist,
    sb, rb, hb, amp, lay_all, wsf, wrf, tx_own, tx_all, sig_all, sig_in, ea, ecol, scol, vs, wsb, w_out,
    symf, tmp, sy, wn, gf, lhs,
    ins, hs, hr, ts, tr, ss, sr, ws, wr, ready,
):
    fetches = [
        pltpu.make_async_copy(source, held, ins.at[i])
        for i, (source, held) in enumerate((
            (lay_any, lay), (uid_any, uid), (power_any, power), (ch_any, ch), (neigh_any, neigh),
            (coup_any, coup), (sym_any, sym), (dft_any, dft), (twist_any, twist),
        ))
    ]
    for fetch in fetches:
        fetch.start()
    me = lax.axis_index("lane")
    mc = lax.axis_index("cell")
    barrier = pltpu.get_barrier_semaphore()

    def lane_peer(d):
        return lax.rem(me + d, LANES)

    def cell_peer(d):
        return lax.rem(mc + d, cells)

    hub = me == 0

    def greet_lane(d, carry):
        peer = lane_peer(d)

        @pl.when(peer != 0)
        def _():
            pl.semaphore_signal(barrier, inc=1, device_id={"lane": peer}, device_id_type=MESH)

        return carry

    def greet_cell(d, _):
        pl.semaphore_signal(barrier, inc=1, device_id={"cell": cell_peer(d)}, device_id_type=MESH)
        return _

    lax.fori_loop(1, LANES, greet_lane, 0)
    @pl.when(hub)
    def _():
        lax.fori_loop(1, cells, greet_cell, 0)


    for fetch in fetches[:3]:
        fetch.wait()
    root = jnp.broadcast_to(jnp.sqrt(power[...]), (LAYERS, W))
    layer = lax.broadcasted_iota(jnp.int32, (LAYERS, W), 0)
    for h in range(2):
        part = slice(h * W, (h + 1) * W)
        picked = jnp.take_along_axis(root, uid[:, part], axis=1, mode="promise_in_bounds")
        granted = layer < lay[:, part]
        spread = swap4([lay[:, part]] * 4)
        for q in range(4):
            lay_all[4 * h + q] = spread[q]
        amplitude = jnp.where(granted, picked, 0.0)
        tx_own[h : h + 1, :] = jnp.sum(amplitude * amplitude, axis=0, keepdims=True) / LAYERS
        spread = swap4([amplitude] * 4)
        for q in range(4):
            amp[4 * h + q] = spread[q]

    def tx_copy(d):
        return pltpu.make_async_remote_copy(
            src_ref=tx_own, dst_ref=tx_all.at[mc], send_sem=ts, recv_sem=tr,
            device_id={"cell": cell_peer(d)}, device_id_type=MESH,
        )

    @pl.when(hub)
    def _():
        pl.semaphore_wait(barrier, cells - 1)
        for d in range(1, cells):
            tx_copy(d).start()

    natural = [pack_tables(lay[:, h * W : (h + 1) * W]) for h in range(2)]
    fetches[3].wait()
    for h in range(2):
        part = slice(h * W, (h + 1) * W)
        for ah in range(2):
            for c in range(2):
                turned = swap4([pack(ch[ah * 4 + g, c, :, part], natural[h]) for g in range(4)])
                first = PACK_ROWS * (2 * ah + c)
                for q in range(4):
                    sb[4 * h + q, first : first + PACK_ROWS, :] = turned[q][:PACK_ROWS]
    own_amp = amp[me]

    def block_copy(src, dst, send, recv, d):
        return pltpu.make_async_remote_copy(
            src_ref=src.at[lane_peer(d)], dst_ref=dst.at[me],
            send_sem=send.at[d - 1], recv_sem=recv.at[d - 1],
            device_id={"lane": lane_peer(d)}, device_id_type=MESH,
        )

    def sigma_copy(z):
        return pltpu.make_async_remote_copy(
            src_ref=sig_all.at[z], dst_ref=sig_in, send_sem=ss.at[z - 1], recv_sem=sr,
            device_id={"lane": z}, device_id_type=MESH,
        )

    far_first = (4, 3, 5, 2, 6, 1, 7)
    @pl.when(hub)
    def _():
        pl.semaphore_wait(ready, LANES - 1)

    @pl.when(me != 0)
    def _():
        pl.semaphore_wait(barrier, LANES - 1)

        pl.semaphore_signal(ready, inc=1, device_id={"lane": 0}, device_id_type=MESH)

    for d in far_first:
        block_copy(sb, rb, hs, hr, d).start()

    @pl.when(hub)
    def _():
        tx_all[mc] = tx_own[...]
        fetches[4].wait()
        fetches[5].wait()

        arrived = tx_all.at[pl.ds(0, cells - 1)]
        pltpu.make_async_copy(arrived, arrived, tr).wait()
        sigma = jnp.full((2, W), NOISE_FLOOR, F32)
        for k in range(neigh.shape[0]):
            sigma = sigma + coup[k, mc] * tx_all[neigh[k, mc]]
        for h in range(2):
            spread = swap4([sigma[h : h + 1, :]] * 4)
            for q in range(4):
                sig_all[4 * h + q] = spread[q]
        for z in far_first:
            sigma_copy(z).start()
        sig_in[...] = sig_all[0]

    @pl.when(me != 0)
    def _():
        fetches[4].wait()
        fetches[5].wait()

    own_tables = pack_tables(lay_all[me])

    def unpack_block(source, z):
        for ah in range(2):
            for c in range(2):
                i = 2 * ah + c
                first = packed_start(i)
                hb[2 * z + ah, c] = unpack(
                    source[z, first : first + 8, :], own_tables, PACK_ROWS * i - first
                )
            hb[2 * z + ah, 2] = hb[2 * z + ah, 0] + hb[2 * z + ah, 1]

    unpack_block(sb, me)
    fetches[6].wait()
    spread_symbols(sym, symf, tmp, sy)

    def take_block(z):
        @pl.when(me != z)
        def _():
            block_copy(sb, rb, hs, hr, lax.rem(me - z + LANES, LANES)).wait_recv()
            unpack_block(rb, z)

    for z in range(1, LANES):
        take_block(z)

    zero = jnp.zeros((8, W), F32)
    for lt in range(2):
        rows = slice(8 * lt, 8 * lt + 8)

        def gram_step(a, acc, rows=rows):
            ar, ai = hb[a, 0, rows, :], hb[a, 1, rows, :]
            out = []
            for m in range(LAYERS):
                br, bi = hb[a, 0, m : m + 1, :], hb[a, 1, m : m + 1, :]
                out.append(acc[2 * m] + (ar * br + ai * bi))
                out.append(acc[2 * m + 1] + (ai * br - ar * bi))
            return tuple(out)

        acc = lax.fori_loop(2, 2 * LANES, gram_step, (zero,) * (2 * LAYERS))
        for m in range(LAYERS):
            ea[0, m, rows, :] = acc[2 * m]
            ea[1, m, rows, :] = acc[2 * m + 1]

    take_block(0)
    for lt in range(2):
        rows = slice(8 * lt, 8 * lt + 8)
        for m in range(LAYERS):
            gr, gi = ea[0, m, rows, :], ea[1, m, rows, :]
            for a in range(2):
                ar, ai = hb[a, 0, rows, :], hb[a, 1, rows, :]
                br, bi = hb[a, 0, m : m + 1, :], hb[a, 1, m : m + 1, :]
                gr = gr + (ar * br + ai * bi)
                gi = gi + (ai * br - ar * bi)
            ea[0, m, rows, :] = total4(gr)
            ea[1, m, rows, :] = total4(gi)

    @pl.when(me != 0)
    def _():
        sigma_copy(1).wait_recv()

    @pl.when(hub)
    def _():
        for z in range(1, LANES):
            sigma_copy(z).wait_send()
        arrived = tx_all.at[pl.ds(0, cells - 1)]
        pltpu.make_async_copy(arrived, arrived, ts).wait()

    sigma = sig_in[...]
    diagonal = jnp.zeros((LAYERS, W), F32)
    for m in range(LAYERS):
        diagonal = diagonal + jnp.where(layer == m, ea[0, m] + sigma, 0.0)
    inv_trace = 1.0 / jnp.sum(diagonal, axis=0, keepdims=True)
    for m in range(LAYERS):
        ea[0, m] = jnp.where(layer == m, 1.0 - (ea[0, m] + sigma) * inv_trace, -ea[0, m] * inv_trace)
        ea[1, m] = -ea[1, m] * inv_trace
        ea[2, m] = ea[0, m] + ea[1, m]
    column = lanes_of((LAYERS, W)) // 32
    for j in range(4):
        for c in range(2):
            ecol[c, j] = pick4([ea[c, 4 * j + g] for g in range(4)])
        scol[0, j] = ecol[0, j] + jnp.where(layer == 4 * j + column, 1.0, 0.0)
        scol[1, j] = ecol[1, j]
        ecol[2, j] = ecol[0, j] + ecol[1, j]
        scol[2, j] = scol[0, j] + scol[1, j]

    def product(ref):
        sums = [[jnp.zeros((LAYERS, W), F32) for j in range(4)] for c in range(3)]
        for k in range(LAYERS):
            for c in range(3):
                left = ea[c, k]
                for j in range(4):
                    sums[c][j] = sums[c][j] + left * ref[c, j, k : k + 1, :]
        real = [sums[0][j] - sums[1][j] for j in range(4)]
        imag = [sums[2][j] - (sums[0][j] + sums[1][j]) for j in range(4)]
        return real, imag

    def put_square(square):
        for c in range(2):
            for j in range(4):
                ecol[c, j] = square[c][j]
        for j in range(4):
            ecol[2, j] = square[0][j] + square[1][j]
        for c in range(3):
            for j in range(4):
                full = spread4(ecol[c, j])
                for g in range(4):
                    ea[c, 4 * j + g] = full[g]

    put_square(product(ecol))

    def level(i, _):
        more = product(scol)
        square = product(ecol)
        for j in range(4):
            for c in range(2):
                scol[c, j] = scol[c, j] + more[c][j]
            scol[2, j] = scol[0, j] + scol[1, j]
        put_square(square)
        return _

    lax.fori_loop(1, 5, level, 0)
    more = product(scol)
    for j in range(4):
        last = [(scol[c, j] + more[c][j]) * inv_trace for c in range(2)]
        for c, part in enumerate(last + [last[0] + last[1]]):
            full = spread4(part)
            for g in range(4):
                ea[c, 4 * j + g] = full[g]

    def apply_step(z, energy):
        sums = [[jnp.zeros((LAYERS, W), F32) for c in range(3)] for ah in range(2)]
        for m in range(LAYERS):
            for c in range(3):
                right = ea[c, m]
                for ah in range(2):
                    sums[ah][c] = sums[ah][c] + hb[2 * z + ah, c, m : m + 1, :] * right
        for ah in range(2):
            vr = sums[ah][0] - sums[ah][1]
            vi = (sums[ah][0] + sums[ah][1]) - sums[ah][2]
            vs[2 * z + ah, 0] = vr
            vs[2 * z + ah, 1] = vi
            energy = energy + (vr * vr + vi * vi)
        return energy

    energy = total4(lax.fori_loop(0, LANES, apply_step, jnp.zeros((LAYERS, W), F32)))
    scale = own_amp / jnp.sqrt(energy + NORM_EPS)

    def round_block(z, target):
        for ah in range(2):
            for c in range(2):
                first = PACK_ROWS * (2 * ah + c)
                wsf[z, first : first + PACK_ROWS, :] = pack(vs[2 * z + ah, c] * scale, own_tables)[:PACK_ROWS]
        target[z] = wsf[z].astype(BF16)

    for d in far_first:
        round_block(lane_peer(d), wsb)
        block_copy(wsb, w_out, ws, wr, d).start()
    round_block(me, w_out)
    natural = [pack_tables(lay[:, h * W : (h + 1) * W]) for h in range(2)]
    for d in far_first[::-1]:
        block_copy(wsb, w_out, ws, wr, d).wait()
    for d in far_first:
        block_copy(sb, rb, hs, hr, d).wait_send()
    for z in range(LANES):
        wrf[z] = w_out[z].astype(F32)

    for h in range(2):
        for ah in range(2):
            for c in range(2):
                i = 2 * ah + c
                first = packed_start(i)
                turned = swap4([wrf[4 * h + q, first : first + 8, :] for q in range(4)])
                for g in range(4):
                    wn[h, ah * 4 + g, c] = unpack(turned[g], natural[h], PACK_ROWS * i - first)
            for g in range(4):
                wn[h, ah * 4 + g, 2] = wn[h, ah * 4 + g, 0] + wn[h, ah * 4 + g, 1]

    for h in range(2):

        def precode(half, _, h=h):
            sums = [[[jnp.zeros((8, W), F32) for i in range(3)] for c in range(3)] for a in range(4)]
            for l in range(LAYERS):
                for c in range(3):
                    first = (c * LAYERS + l) * 24
                    right = [sy[h, first + 8 * i : first + 8 * i + 8, :] for i in range(3)]
                    for a in range(4):
                        left = wn[h, 4 * half + a, c, l : l + 1, :]
                        for i in range(3):
                            sums[a][c][i] = sums[a][c][i] + left * right[i]
            for a in range(4):
                for i in range(3):
                    p0, p1, p2 = sums[a][0][i], sums[a][1][i], sums[a][2][i]
                    sums[a][0][i] = p0 - p1
                    sums[a][1][i] = p2 - (p0 + p1)
            for a in range(4):
                for c in range(2):
                    for i in range(3):
                        gf[c, h, pl.ds(64 * i + 4 * half + a, 8, stride=8), :] = sums[a][c][i]
            return _

        lax.fori_loop(0, 2, precode, 0)

    for c in range(2):
        for h in range(2):
            value = gf[c, h]
            high = value.astype(BF16)
            cols = slice(c * PRBS + h * W, c * PRBS + (h + 1) * W)
            lhs[:, cols] = high

    fetches[7].wait()
    fetches[8].wait()

    def section(nt, _):
        result = jnp.dot(lhs[...], dft[nt], preferred_element_type=F32)
        for s in range(SYMS):
            part = [[None, None] for _ in range(4)]
            for k in range(SUBC):
                row = (s * SUBC + k) * 8
                tr, ti = result[row : row + 8, 0:W], result[row : row + 8, W : 2 * W]
                cr, ci = twist[nt, k : k + 1, :], twist[nt, SUBC + k : SUBC + k + 1, :]
                ur, ui = tr * cr - ti * ci, tr * ci + ti * cr
                held = part[k % 4]
                held[0] = ur if held[0] is None else held[0] + ur
                held[1] = ui if held[1] is None else held[1] + ui
            (ar, ai), (br, bi), (cr, ci), (dr, di) = part
            pr, pi, mr, mi = ar + cr, ai + ci, ar - cr, ai - ci
            qr, qi, nr, ni = br + dr, bi + di, br - dr, bi - di
            outs = ((pr + qr, pi + qi), (mr - ni, mi + nr), (pr - qr, pi - qi), (mr + ni, mi - nr))
            for n2 in range(4):
                for c in range(2):
                    out[pl.ds(c * 64 + (n2 * 8 + nt) * 2 + s, 8, stride=128), :] = outs[n2][c]
        return _

    lax.fori_loop(0, 8, section, 0)


def ofdm_tables():
    p = np.arange(PRBS)[:, None]
    n = np.arange(1024)[None, :]
    angle = 2.0 * math.pi * ((3 * p * n) % 1024) / 1024
    cos, sin = np.cos(angle), np.sin(angle)
    real = np.concatenate([cos, -sin], 0).reshape(2 * PRBS, 8, 1, W)
    imag = np.concatenate([sin, cos], 0).reshape(2 * PRBS, 8, 1, W)
    dft = np.concatenate([real, imag], 2).reshape(2 * PRBS, 8, 2 * W).transpose(1, 0, 2)
    k = np.arange(SUBC)[:, None]
    angle = 2.0 * math.pi * (((k - 1536) * n) % NFFT) / NFFT
    twist = np.concatenate([np.cos(angle), np.sin(angle)], 0) / math.sqrt(NFFT)
    twist = twist.reshape(2 * SUBC, 8, W).transpose(1, 0, 2)
    return jnp.asarray(dft, BF16), jnp.asarray(twist, F32)


def slot(cells, channel, symbols, layers, user_ids, user_power, neighbours, coupling):
    dft, twist = ofdm_tables()
    args = (channel, symbols, layers, user_ids, user_power, neighbours, coupling, dft, twist)
    block = (2 * LANES, 2, LAYERS, W)
    packed = (LANES, 4 * PACK_ROWS, W)
    dma = pltpu.SemaphoreType.DMA
    held = [(pltpu.SMEM if i in (5, 6) else pltpu.VMEM)(x.shape, x.dtype) for i, x in enumerate(args)]
    return pl.pallas_call(
        functools.partial(slot_kernel, cells),
        out_shape=pltpu.VMEM((1024, W), F32),
        in_specs=[pl.BlockSpec(memory_space=pl.ANY)] * len(args),
        out_specs=pl.BlockSpec(memory_space=pltpu.VMEM),
        scratch_shapes=held + [
            pltpu.VMEM(packed, F32),
            pltpu.VMEM(packed, F32),
            pltpu.VMEM((2 * LANES, 3, LAYERS, W), F32),
            pltpu.VMEM((LANES, LAYERS, W), F32),
            pltpu.VMEM((LANES, 1, W), jnp.int32),
            pltpu.VMEM(packed, F32),
            pltpu.VMEM(packed, F32),
            pltpu.VMEM((2, W), F32),
            pltpu.VMEM((cells, 2, W), F32),
            pltpu.VMEM((LANES, 1, W), F32),
            pltpu.VMEM((1, W), F32),
            pltpu.VMEM((3, LAYERS, LAYERS, W), F32),
            pltpu.VMEM((3, 4, LAYERS, W), F32),
            pltpu.VMEM((3, 4, LAYERS, W), F32),
            pltpu.VMEM(block, F32),
            pltpu.VMEM(packed, BF16),
            pltpu.VMEM(packed, BF16),
            pltpu.VMEM((64, 3072), F32),
            pltpu.VMEM((8, 64, 384), F32),
            pltpu.VMEM((2, 1152, W), F32),
            pltpu.VMEM((2, 8, 3, LAYERS, W), F32),
            pltpu.VMEM((2, 2, 192, W), F32),
            pltpu.VMEM((192, 512), BF16),
            dma((len(args),)),
            dma((LANES - 1,)),
            dma((LANES - 1,)),
            dma,
            dma,
            dma((LANES - 1,)),
            dma,
            dma((LANES - 1,)),
            dma((LANES - 1,)),
            pltpu.SemaphoreType.REGULAR,
        ],
        compiler_params=pltpu.CompilerParams(collective_id=0, has_side_effects=True),
        name="slot",
    )(*args)


def per_device(cells, channel, symbols, layers, user_ids, user_power, neighbours, coupling):
    samples = slot(
        cells, channel[0], symbols[0].reshape(2 * LAYERS, SYMS, 3072), layers, user_ids[0], user_power,
        neighbours.T, coupling.T,
    )
    samples = samples.reshape(8, 2, 32, SYMS, W).transpose(0, 1, 3, 2, 4)
    return samples.reshape(1, 8, 2, SYMS, NFFT)


def solution(mesh):
    in_specs = (
        P("cell", "lane", None, None, None),
        P("cell", None, None, None, None),
        P("cell", None),
        P("cell", None, None),
        P("cell", None),
        P(),
        P(),
    )
    out_specs = P("cell", "lane", None, None, None)
    return jax.shard_map(
        functools.partial(per_device, mesh.shape["cell"]),
        mesh=mesh, in_specs=in_specs, out_specs=out_specs, check_vma=False,
    )
```

```python
import functools
import math

import jax
import jax.numpy as jnp
import numpy as np
from jax import lax
from jax.experimental import pallas as pl
from jax.experimental.pallas import tpu as pltpu
from jax.sharding import PartitionSpec as P

MESH = pl.DeviceIdType.MESH
NFFT = 4096
PRBS = 256
SUBC = 12
SYMS = 2
LAYERS = 16
NORM_EPS = 1e-06
NOISE_FLOOR = 0.05
LANES = 8
W = 128
F32 = jnp.float32
BF16 = jnp.bfloat16


def lanes_of(shape):
    return lax.broadcasted_iota(jnp.int32, shape, len(shape) - 1)


def swap4(x):
    lane = lanes_of(x[0].shape)
    low_half = lane < 64
    even = lax.rem(lane, 64) < 32
    y0 = jnp.where(low_half, x[0], pltpu.roll(x[2], 64, 1))
    y2 = jnp.where(low_half, pltpu.roll(x[0], 64, 1), x[2])
    y1 = jnp.where(low_half, x[1], pltpu.roll(x[3], 64, 1))
    y3 = jnp.where(low_half, pltpu.roll(x[1], 64, 1), x[3])
    z0 = jnp.where(even, y0, pltpu.roll(y1, 32, 1))
    z1 = jnp.where(even, pltpu.roll(y0, 96, 1), y1)
    z2 = jnp.where(even, y2, pltpu.roll(y3, 32, 1))
    z3 = jnp.where(even, pltpu.roll(y2, 96, 1), y3)
    return [z0, z1, z2, z3]


def pick4(x):
    lane = lanes_of(x[0].shape)
    return jnp.where(
        lane < 64,
        jnp.where(lane < 32, x[0], x[1]),
        jnp.where(lane < 96, x[2], x[3]),
    )


def spread4(x):
    r = [x, pltpu.roll(x, 32, 1), pltpu.roll(x, 64, 1), pltpu.roll(x, 96, 1)]
    return [pick4([r[(h - g) % 4] for h in range(4)]) for g in range(4)]


def total4(x):
    x = x + pltpu.roll(x, 64, 1)
    return x + pltpu.roll(x, 32, 1)


def spread_symbols(sym, symf, tmp, sy):
    def widen(lc, _):
        pair = sym[lc].astype(F32)
        row = lax.rem(lc, 2) * LAYERS + lc // 2
        symf[pl.ds(row, 1), :] = pair[0:1, :]
        symf[pl.ds(2 * LAYERS + row, 1), :] = pair[1:2, :]
        return _

    lax.fori_loop(0, 2 * LAYERS, widen, 0)
    j = lax.broadcasted_iota(jnp.int32, (384, 384), 0)
    o = lax.broadcasted_iota(jnp.int32, (384, 384), 1)
    source = SUBC * lax.rem(o, 32) + o // 32
    order = jnp.where(j == source, 1.0, 0.0).astype(BF16)
    for z in range(8):
        tmp[z] = jnp.dot(symf[:, 384 * z : 384 * (z + 1)].astype(BF16), order, preferred_element_type=F32)
    for h in range(2):
        for t in range(3):
            turned = swap4([tmp[4 * h + q, :, W * t : W * (t + 1)] for q in range(4)])
            for kk in range(4):
                k = 4 * t + kk
                for s in range(SYMS):
                    parts = [turned[kk][s * 32 + b * 8 : s * 32 + b * 8 + 8, :] for b in range(4)]
                    parts += [parts[0] + parts[2], parts[1] + parts[3]]
                    for b, part in enumerate(parts):
                        sy[h, pl.ds(b * 8 * 24 + s * SUBC + k, 8, stride=24), :] = part


GROUP = 8
PACK_ROWS = 6


def group_total(x):
    position = lax.rem(lanes_of(x.shape), GROUP)
    for step in (1, 2, 4):
        upper = lax.rem(position // step, 2) == 1
        x = x + jnp.where(upper, pltpu.roll(x, step, 1), pltpu.roll(x, W - step, 1))
    return x


def pack_tables(count):
    shape = (LAYERS, W)
    layer = lax.broadcasted_iota(jnp.int32, shape, 0)
    lane = lanes_of(shape)
    position = lax.rem(lane, GROUP)
    base = lane - position
    granted = layer < count
    one = jnp.where(granted, 1, 0)
    rank = one
    for step in (1, 2, 4):
        rank = rank + jnp.where(position >= step, pltpu.roll(rank, step, 1), 0)
    rank = rank - one
    number = group_total(one)
    offset = group_total(jnp.minimum(count, layer))
    target = lax.rem(offset + rank, GROUP)
    unpack_lane = base + target
    turn = lax.rem(position - offset + LAYERS * GROUP, GROUP)
    unpack_row = jnp.minimum((offset + turn) // GROUP, PACK_ROWS - 1)
    marked = jnp.where(granted, target, GROUP)
    pack_lane = lane
    for step in range(GROUP):
        if step == 0:
            seen = marked
        else:
            seen = jnp.where(
                position + step < GROUP, pltpu.roll(marked, W - step, 1), pltpu.roll(marked, GROUP - step, 1)
            )
        source = base + lax.rem(position + step, GROUP)
        pack_lane = jnp.where(seen == position, source, pack_lane)
    row = lax.broadcasted_iota(jnp.int32, (8, W), 0)
    pack_layer = jnp.zeros((8, W), jnp.int32)
    for r in range(PACK_ROWS):
        passed = jnp.where(offset + number <= GROUP * r + position, 1, 0)
        level = jnp.minimum(jnp.sum(passed, axis=0, keepdims=True), LAYERS - 1)
        pack_layer = jnp.where(row == r, level, pack_layer)
    return granted, pack_lane, pack_layer, unpack_row, unpack_lane


def along(x, index, axis):
    return jnp.take_along_axis(x, index, axis=axis, mode="promise_in_bounds")


def pack(x, tables):
    pack_lane, pack_layer = tables[1], tables[2]
    turned = [along(x[8 * i : 8 * i + 8], pack_lane[8 * i : 8 * i + 8], 1) for i in range(2)]
    within = lax.rem(pack_layer, 8)
    return jnp.where(pack_layer < 8, along(turned[0], within, 0), along(turned[1], within, 0))


def unpack(x, tables, first=0):
    granted, unpack_row, unpack_lane = tables[0], tables[3] + first, tables[4]
    parts = []
    for i in range(2):
        rows = slice(8 * i, 8 * i + 8)
        parts.append(along(along(x, unpack_row[rows], 0), unpack_lane[rows], 1))
    return jnp.where(granted, jnp.concatenate(parts, axis=0), 0.0)


def packed_start(i):
    return min(PACK_ROWS * i, 4 * PACK_ROWS - 8)


def slot_kernel(
    cells, ch_any, sym_any, lay_any, uid_any, power_any, neigh_any, coup_any, dft_any, twist_any, out,
    ch, sym, lay, uid, power, neigh, coup, dft, twist,
    sb, rb, hb, amp, lay_all, wsf, wrf, tx_own, tx_all, sig_all, sig_in, ea, ecol, scol, vs, wsb, w_out,
    symf, tmp, sy, wn, gf, lhs,
    ins, hs, hr, ts, tr, ss, sr, ws, wr, ready,
):
    fetches = [
        pltpu.make_async_copy(source, held, ins.at[i])
        for i, (source, held) in enumerate((
            (lay_any, lay), (uid_any, uid), (power_any, power), (ch_any, ch), (neigh_any, neigh),
            (coup_any, coup), (sym_any, sym), (dft_any, dft), (twist_any, twist),
        ))
    ]
    for fetch in fetches:
        fetch.start()
    me = lax.axis_index("lane")
    mc = lax.axis_index("cell")
    barrier = pltpu.get_barrier_semaphore()

    def lane_peer(d):
        return lax.rem(me + d, LANES)

    def cell_peer(d):
        return lax.rem(mc + d, cells)

    hub = me == 0

    def greet_lane(d, carry):
        peer = lane_peer(d)

        @pl.when(peer != 0)
        def _():
            pl.semaphore_signal(barrier, inc=1, device_id={"lane": peer}, device_id_type=MESH)

        return carry

    def greet_cell(d, _):
        pl.semaphore_signal(barrier, inc=1, device_id={"cell": cell_peer(d)}, device_id_type=MESH)
        return _

    lax.fori_loop(1, LANES, greet_lane, 0)
    @pl.when(hub)
    def _():
        lax.fori_loop(1, cells, greet_cell, 0)


    for fetch in fetches[:3]:
        fetch.wait()
    root = jnp.broadcast_to(jnp.sqrt(power[...]), (LAYERS, W))
    layer = lax.broadcasted_iota(jnp.int32, (LAYERS, W), 0)
    for h in range(2):
        part = slice(h * W, (h + 1) * W)
        picked = jnp.take_along_axis(root, uid[:, part], axis=1, mode="promise_in_bounds")
        granted = layer < lay[:, part]
        spread = swap4([lay[:, part]] * 4)
        for q in range(4):
            lay_all[4 * h + q] = spread[q]
        amplitude = jnp.where(granted, picked, 0.0)
        tx_own[h : h + 1, :] = jnp.sum(amplitude * amplitude, axis=0, keepdims=True) / LAYERS
        spread = swap4([amplitude] * 4)
        for q in range(4):
            amp[4 * h + q] = spread[q]

    def tx_copy(d):
        return pltpu.make_async_remote_copy(
            src_ref=tx_own, dst_ref=tx_all.at[mc], send_sem=ts, recv_sem=tr,
            device_id={"cell": cell_peer(d)}, device_id_type=MESH,
        )

    @pl.when(hub)
    def _():
        pl.semaphore_wait(barrier, cells - 1)
        for d in range(1, cells):
            tx_copy(d).start()

    natural = [pack_tables(lay[:, h * W : (h + 1) * W]) for h in range(2)]
    fetches[3].wait()
    for h in range(2):
        part = slice(h * W, (h + 1) * W)
        for ah in range(2):
            for c in range(2):
                turned = swap4([pack(ch[ah * 4 + g, c, :, part], natural[h]) for g in range(4)])
                first = PACK_ROWS * (2 * ah + c)
                for q in range(4):
                    sb[4 * h + q, first : first + PACK_ROWS, :] = turned[q][:PACK_ROWS]
    own_amp = amp[me]

    def block_copy(src, dst, send, recv, d):
        return pltpu.make_async_remote_copy(
            src_ref=src.at[lane_peer(d)], dst_ref=dst.at[me],
            send_sem=send.at[d - 1], recv_sem=recv.at[d - 1],
            device_id={"lane": lane_peer(d)}, device_id_type=MESH,
        )

    def sigma_copy(z):
        return pltpu.make_async_remote_copy(
            src_ref=sig_all.at[z], dst_ref=sig_in, send_sem=ss.at[z - 1], recv_sem=sr,
            device_id={"lane": z}, device_id_type=MESH,
        )

    far_first = (4, 3, 5, 2, 6, 1, 7)
    @pl.when(hub)
    def _():
        pl.semaphore_wait(ready, LANES - 1)

    @pl.when(me != 0)
    def _():
        pl.semaphore_wait(barrier, LANES - 1)

        pl.semaphore_signal(ready, inc=1, device_id={"lane": 0}, device_id_type=MESH)

    for d in far_first:
        block_copy(sb, rb, hs, hr, d).start()

    @pl.when(hub)
    def _():
        tx_all[mc] = tx_own[...]
        fetches[4].wait()
        fetches[5].wait()

        arrived = tx_all.at[pl.ds(0, cells - 1)]
        pltpu.make_async_copy(arrived, arrived, tr).wait()
        sigma = jnp.full((2, W), NOISE_FLOOR, F32)
        for k in range(neigh.shape[0]):
            sigma = sigma + coup[k, mc] * tx_all[neigh[k, mc]]
        for h in range(2):
            spread = swap4([sigma[h : h + 1, :]] * 4)
            for q in range(4):
                sig_all[4 * h + q] = spread[q]
        for z in far_first:
            sigma_copy(z).start()
        sig_in[...] = sig_all[0]

    @pl.when(me != 0)
    def _():
        fetches[4].wait()
        fetches[5].wait()

    own_tables = pack_tables(lay_all[me])

    def unpack_block(source, z):
        for ah in range(2):
            for c in range(2):
                i = 2 * ah + c
                first = packed_start(i)
                hb[2 * z + ah, c] = unpack(
                    source[z, first : first + 8, :], own_tables, PACK_ROWS * i - first
                )
            hb[2 * z + ah, 2] = hb[2 * z + ah, 0] + hb[2 * z + ah, 1]

    unpack_block(sb, me)
    fetches[6].wait()
    spread_symbols(sym, symf, tmp, sy)

    def take_block(z):
        @pl.when(me != z)
        def _():
            block_copy(sb, rb, hs, hr, lax.rem(me - z + LANES, LANES)).wait_recv()
            unpack_block(rb, z)

    for z in range(1, LANES):
        take_block(z)

    zero = jnp.zeros((8, W), F32)
    for lt in range(2):
        rows = slice(8 * lt, 8 * lt + 8)

        def gram_step(a, acc, rows=rows):
            ar, ai = hb[a, 0, rows, :], hb[a, 1, rows, :]
            out = []
            for m in range(LAYERS):
                br, bi = hb[a, 0, m : m + 1, :], hb[a, 1, m : m + 1, :]
                out.append(acc[2 * m] + (ar * br + ai * bi))
                out.append(acc[2 * m + 1] + (ai * br - ar * bi))
            return tuple(out)

        acc = lax.fori_loop(2, 2 * LANES, gram_step, (zero,) * (2 * LAYERS))
        for m in range(LAYERS):
            ea[0, m, rows, :] = acc[2 * m]
            ea[1, m, rows, :] = acc[2 * m + 1]

    take_block(0)
    for lt in range(2):
        rows = slice(8 * lt, 8 * lt + 8)
        for m in range(LAYERS):
            gr, gi = ea[0, m, rows, :], ea[1, m, rows, :]
            for a in range(2):
                ar, ai = hb[a, 0, rows, :], hb[a, 1, rows, :]
                br, bi = hb[a, 0, m : m + 1, :], hb[a, 1, m : m + 1, :]
                gr = gr + (ar * br + ai * bi)
                gi = gi + (ai * br - ar * bi)
            ea[0, m, rows, :] = total4(gr)
            ea[1, m, rows, :] = total4(gi)

    @pl.when(me != 0)
    def _():
        sigma_copy(1).wait_recv()

    @pl.when(hub)
    def _():
        for z in range(1, LANES):
            sigma_copy(z).wait_send()
        arrived = tx_all.at[pl.ds(0, cells - 1)]
        pltpu.make_async_copy(arrived, arrived, ts).wait()

    sigma = sig_in[...]
    diagonal = jnp.zeros((LAYERS, W), F32)
    for m in range(LAYERS):
        diagonal = diagonal + jnp.where(layer == m, ea[0, m] + sigma, 0.0)
    inv_trace = 1.0 / jnp.sum(diagonal, axis=0, keepdims=True)
    for m in range(LAYERS):
        ea[0, m] = jnp.where(layer == m, 1.0 - (ea[0, m] + sigma) * inv_trace, -ea[0, m] * inv_trace)
        ea[1, m] = -ea[1, m] * inv_trace
        ea[2, m] = ea[0, m] + ea[1, m]
    column = lanes_of((LAYERS, W)) // 32
    for j in range(4):
        for c in range(2):
            ecol[c, j] = pick4([ea[c, 4 * j + g] for g in range(4)])
        scol[0, j] = ecol[0, j] + jnp.where(layer == 4 * j + column, 1.0, 0.0)
        scol[1, j] = ecol[1, j]
        ecol[2, j] = ecol[0, j] + ecol[1, j]
        scol[2, j] = scol[0, j] + scol[1, j]

    def products(refs):
        sums = [[[jnp.zeros((LAYERS, W), F32) for j in range(4)] for c in range(3)] for _ in refs]
        for c in range(3):
            for k in range(LAYERS):
                left = ea[c, k]
                for ref, held in zip(refs, sums):
                    for j in range(4):
                        held[c][j] = held[c][j] + left * ref[c, j, k : k + 1, :]
        return [
            (
                [held[0][j] - held[1][j] for j in range(4)],
                [held[2][j] - (held[0][j] + held[1][j]) for j in range(4)],
            )
            for held in sums
        ]

    def put_square(square):
        for c in range(2):
            for j in range(4):
                ecol[c, j] = square[c][j]
        for j in range(4):
            ecol[2, j] = square[0][j] + square[1][j]
        for j in range(4):
            real, imag = spread4(square[0][j]), spread4(square[1][j])
            for g in range(4):
                ea[0, 4 * j + g] = real[g]
                ea[1, 4 * j + g] = imag[g]
                ea[2, 4 * j + g] = real[g] + imag[g]

    put_square(products([ecol])[0])

    def level(i, _):
        more, square = products([scol, ecol])
        for j in range(4):
            for c in range(2):
                scol[c, j] = scol[c, j] + more[c][j]
            scol[2, j] = scol[0, j] + scol[1, j]
        put_square(square)
        return _

    lax.fori_loop(1, 5, level, 0)
    (more,) = products([scol])
    for j in range(4):
        last = [(scol[c, j] + more[c][j]) * inv_trace for c in range(2)]
        real, imag = spread4(last[0]), spread4(last[1])
        for g in range(4):
            ea[0, 4 * j + g] = real[g]
            ea[1, 4 * j + g] = imag[g]
            ea[2, 4 * j + g] = real[g] + imag[g]

    def apply_step(z, energy):
        sums = [[jnp.zeros((LAYERS, W), F32) for c in range(3)] for a in range(4)]
        for c in range(3):
            for m in range(LAYERS):
                right = ea[c, m]
                for a in range(4):
                    sums[a][c] = sums[a][c] + hb[4 * z + a, c, m : m + 1, :] * right
        for a in range(4):
            vr = sums[a][0] - sums[a][1]
            vi = (sums[a][0] + sums[a][1]) - sums[a][2]
            vs[4 * z + a, 0] = vr
            vs[4 * z + a, 1] = vi
            energy = energy + (vr * vr + vi * vi)
        return energy

    energy = total4(lax.fori_loop(0, LANES // 2, apply_step, jnp.zeros((LAYERS, W), F32)))
    scale = own_amp / jnp.sqrt(energy + NORM_EPS)

    def round_block(z, target):
        for ah in range(2):
            for c in range(2):
                first = PACK_ROWS * (2 * ah + c)
                wsf[z, first : first + PACK_ROWS, :] = pack(vs[2 * z + ah, c] * scale, own_tables)[:PACK_ROWS]
        target[z] = wsf[z].astype(BF16)

    for d in far_first:
        round_block(lane_peer(d), wsb)
        block_copy(wsb, w_out, ws, wr, d).start()
    round_block(me, w_out)
    natural = [pack_tables(lay[:, h * W : (h + 1) * W]) for h in range(2)]
    for d in far_first[::-1]:
        block_copy(wsb, w_out, ws, wr, d).wait()
    for d in far_first:
        block_copy(sb, rb, hs, hr, d).wait_send()
    for z in range(LANES):
        wrf[z] = w_out[z].astype(F32)

    for h in range(2):
        for ah in range(2):
            for c in range(2):
                i = 2 * ah + c
                first = packed_start(i)
                turned = swap4([wrf[4 * h + q, first : first + 8, :] for q in range(4)])
                for g in range(4):
                    wn[h, ah * 4 + g, c] = unpack(turned[g], natural[h], PACK_ROWS * i - first)
            for g in range(4):
                wn[h, ah * 4 + g, 2] = wn[h, ah * 4 + g, 0] + wn[h, ah * 4 + g, 1]

    for h in range(2):

        def precode(half, _, h=h):
            sums = [[[jnp.zeros((8, W), F32) for i in range(3)] for c in range(3)] for a in range(4)]
            for l in range(LAYERS):
                for c in range(3):
                    first = (c * LAYERS + l) * 24
                    right = [sy[h, first + 8 * i : first + 8 * i + 8, :] for i in range(3)]
                    for a in range(4):
                        left = wn[h, 4 * half + a, c, l : l + 1, :]
                        for i in range(3):
                            sums[a][c][i] = sums[a][c][i] + left * right[i]
            for a in range(4):
                for i in range(3):
                    p0, p1, p2 = sums[a][0][i], sums[a][1][i], sums[a][2][i]
                    sums[a][0][i] = p0 - p1
                    sums[a][1][i] = p2 - (p0 + p1)
            for a in range(4):
                for c in range(2):
                    for i in range(3):
                        gf[c, h, pl.ds(64 * i + 4 * half + a, 8, stride=8), :] = sums[a][c][i]
            return _

        lax.fori_loop(0, 2, precode, 0)

    for c in range(2):
        for h in range(2):
            value = gf[c, h]
            high = value.astype(BF16)
            cols = slice(c * PRBS + h * W, c * PRBS + (h + 1) * W)
            lhs[:, cols] = high

    fetches[7].wait()
    fetches[8].wait()

    def section(nt):
        result = jnp.dot(lhs[...], dft[nt], preferred_element_type=F32)
        for s in range(SYMS):
            part = [[None, None] for _ in range(4)]
            for k in range(SUBC):
                row = (s * SUBC + k) * 8
                tr, ti = result[row : row + 8, 0:W], result[row : row + 8, W : 2 * W]
                cr, ci = twist[nt, k : k + 1, :], twist[nt, SUBC + k : SUBC + k + 1, :]
                ur, ui = tr * cr - ti * ci, tr * ci + ti * cr
                held = part[k % 4]
                held[0] = ur if held[0] is None else held[0] + ur
                held[1] = ui if held[1] is None else held[1] + ui
            (ar, ai), (br, bi), (cr, ci), (dr, di) = part
            pr, pi, mr, mi = ar + cr, ai + ci, ar - cr, ai - ci
            qr, qi, nr, ni = br + dr, bi + di, br - dr, bi - di
            outs = ((pr + qr, pi + qi), (mr - ni, mi + nr), (pr - qr, pi - qi), (mr + ni, mi - nr))
            for n2 in range(4):
                for c in range(2):
                    out[pl.ds(c * 64 + (n2 * 8 + nt) * 2 + s, 8, stride=128), :] = outs[n2][c]

    def sections(i, _):
        for step in range(4):
            section(4 * i + step)
        return _

    lax.fori_loop(0, 2, sections, 0)


def ofdm_tables():
    p = np.arange(PRBS)[:, None]
    n = np.arange(1024)[None, :]
    angle = 2.0 * math.pi * ((3 * p * n) % 1024) / 1024
    cos, sin = np.cos(angle), np.sin(angle)
    real = np.concatenate([cos, -sin], 0).reshape(2 * PRBS, 8, 1, W)
    imag = np.concatenate([sin, cos], 0).reshape(2 * PRBS, 8, 1, W)
    dft = np.concatenate([real, imag], 2).reshape(2 * PRBS, 8, 2 * W).transpose(1, 0, 2)
    k = np.arange(SUBC)[:, None]
    angle = 2.0 * math.pi * (((k - 1536) * n) % NFFT) / NFFT
    twist = np.concatenate([np.cos(angle), np.sin(angle)], 0) / math.sqrt(NFFT)
    twist = twist.reshape(2 * SUBC, 8, W).transpose(1, 0, 2)
    return jnp.asarray(dft, BF16), jnp.asarray(twist, F32)


def slot(cells, channel, symbols, layers, user_ids, user_power, neighbours, coupling):
    dft, twist = ofdm_tables()
    args = (channel, symbols, layers, user_ids, user_power, neighbours, coupling, dft, twist)
    block = (2 * LANES, 2, LAYERS, W)
    packed = (LANES, 4 * PACK_ROWS, W)
    dma = pltpu.SemaphoreType.DMA
    held = [(pltpu.SMEM if i in (5, 6) else pltpu.VMEM)(x.shape, x.dtype) for i, x in enumerate(args)]
    return pl.pallas_call(
        functools.partial(slot_kernel, cells),
        out_shape=pltpu.VMEM((1024, W), F32),
        in_specs=[pl.BlockSpec(memory_space=pl.ANY)] * len(args),
        out_specs=pl.BlockSpec(memory_space=pltpu.VMEM),
        scratch_shapes=held + [
            pltpu.VMEM(packed, F32),
            pltpu.VMEM(packed, F32),
            pltpu.VMEM((2 * LANES, 3, LAYERS, W), F32),
            pltpu.VMEM((LANES, LAYERS, W), F32),
            pltpu.VMEM((LANES, 1, W), jnp.int32),
            pltpu.VMEM(packed, F32),
            pltpu.VMEM(packed, F32),
            pltpu.VMEM((2, W), F32),
            pltpu.VMEM((cells, 2, W), F32),
            pltpu.VMEM((LANES, 1, W), F32),
            pltpu.VMEM((1, W), F32),
            pltpu.VMEM((3, LAYERS, LAYERS, W), F32),
            pltpu.VMEM((3, 4, LAYERS, W), F32),
            pltpu.VMEM((3, 4, LAYERS, W), F32),
            pltpu.VMEM(block, F32),
            pltpu.VMEM(packed, BF16),
            pltpu.VMEM(packed, BF16),
            pltpu.VMEM((64, 3072), F32),
            pltpu.VMEM((8, 64, 384), F32),
            pltpu.VMEM((2, 1152, W), F32),
            pltpu.VMEM((2, 8, 3, LAYERS, W), F32),
            pltpu.VMEM((2, 2, 192, W), F32),
            pltpu.VMEM((192, 512), BF16),
            dma((len(args),)),
            dma((LANES - 1,)),
            dma((LANES - 1,)),
            dma,
            dma,
            dma((LANES - 1,)),
            dma,
            dma((LANES - 1,)),
            dma((LANES - 1,)),
            pltpu.SemaphoreType.REGULAR,
        ],
        compiler_params=pltpu.CompilerParams(collective_id=0, has_side_effects=True),
        name="slot",
    )(*args)


def per_device(cells, channel, symbols, layers, user_ids, user_power, neighbours, coupling):
    samples = slot(
        cells, channel[0], symbols[0].reshape(2 * LAYERS, SYMS, 3072), layers, user_ids[0], user_power,
        neighbours.T, coupling.T,
    )
    samples = samples.reshape(8, 2, 32, SYMS, W).transpose(0, 1, 3, 2, 4)
    return samples.reshape(1, 8, 2, SYMS, NFFT)


def solution(mesh):
    in_specs = (
        P("cell", "lane", None, None, None),
        P("cell", None, None, None, None),
        P("cell", None),
        P("cell", None, None),
        P("cell", None),
        P(),
        P(),
    )
    out_specs = P("cell", "lane", None, None, None)
    return jax.shard_map(
        functools.partial(per_device, mesh.shape["cell"]),
        mesh=mesh, in_specs=in_specs, out_specs=out_specs, check_vma=False,
    )
```

```python
import functools
import math

import jax
import jax.numpy as jnp
import numpy as np
from jax import lax
from jax.experimental import pallas as pl
from jax.experimental.pallas import tpu as pltpu
from jax.sharding import PartitionSpec as P

MESH = pl.DeviceIdType.MESH
NFFT = 4096
PRBS = 256
SUBC = 12
SYMS = 2
LAYERS = 16
NORM_EPS = 1e-06
NOISE_FLOOR = 0.05
LANES = 8
W = 128
F32 = jnp.float32
BF16 = jnp.bfloat16


def lanes_of(shape):
    return lax.broadcasted_iota(jnp.int32, shape, len(shape) - 1)


def swap4(x):
    lane = lanes_of(x[0].shape)
    low_half = lane < 64
    even = lax.rem(lane, 64) < 32
    y0 = jnp.where(low_half, x[0], pltpu.roll(x[2], 64, 1))
    y2 = jnp.where(low_half, pltpu.roll(x[0], 64, 1), x[2])
    y1 = jnp.where(low_half, x[1], pltpu.roll(x[3], 64, 1))
    y3 = jnp.where(low_half, pltpu.roll(x[1], 64, 1), x[3])
    z0 = jnp.where(even, y0, pltpu.roll(y1, 32, 1))
    z1 = jnp.where(even, pltpu.roll(y0, 96, 1), y1)
    z2 = jnp.where(even, y2, pltpu.roll(y3, 32, 1))
    z3 = jnp.where(even, pltpu.roll(y2, 96, 1), y3)
    return [z0, z1, z2, z3]


def pick4(x):
    lane = lanes_of(x[0].shape)
    return jnp.where(
        lane < 64,
        jnp.where(lane < 32, x[0], x[1]),
        jnp.where(lane < 96, x[2], x[3]),
    )


def spread4(x):
    r = [x, pltpu.roll(x, 32, 1), pltpu.roll(x, 64, 1), pltpu.roll(x, 96, 1)]
    return [pick4([r[(h - g) % 4] for h in range(4)]) for g in range(4)]


def total4(x):
    x = x + pltpu.roll(x, 64, 1)
    return x + pltpu.roll(x, 32, 1)


def spread_symbols(sym, symf, tmp, sy):
    def widen(lc, _):
        pair = sym[lc].astype(F32)
        row = lax.rem(lc, 2) * LAYERS + lc // 2
        symf[pl.ds(row, 1), :] = pair[0:1, :]
        symf[pl.ds(2 * LAYERS + row, 1), :] = pair[1:2, :]
        return _

    lax.fori_loop(0, 2 * LAYERS, widen, 0)
    j = lax.broadcasted_iota(jnp.int32, (384, 384), 0)
    o = lax.broadcasted_iota(jnp.int32, (384, 384), 1)
    source = SUBC * lax.rem(o, 32) + o // 32
    order = jnp.where(j == source, 1.0, 0.0).astype(BF16)
    for z in range(8):
        tmp[z] = jnp.dot(symf[:, 384 * z : 384 * (z + 1)].astype(BF16), order, preferred_element_type=F32)
    for h in range(2):
        for t in range(3):
            turned = swap4([tmp[4 * h + q, :, W * t : W * (t + 1)] for q in range(4)])
            for kk in range(4):
                k = 4 * t + kk
                for s in range(SYMS):
                    parts = [turned[kk][s * 32 + b * 8 : s * 32 + b * 8 + 8, :] for b in range(4)]
                    parts += [parts[0] + parts[2], parts[1] + parts[3]]
                    for b, part in enumerate(parts):
                        sy[h, pl.ds(b * 8 * 24 + s * SUBC + k, 8, stride=24), :] = part


GROUP = 8
PACK_ROWS = 6


def group_total(x):
    position = lax.rem(lanes_of(x.shape), GROUP)
    for step in (1, 2, 4):
        upper = lax.rem(position // step, 2) == 1
        x = x + jnp.where(upper, pltpu.roll(x, step, 1), pltpu.roll(x, W - step, 1))
    return x


def pack_tables(count):
    shape = (LAYERS, W)
    layer = lax.broadcasted_iota(jnp.int32, shape, 0)
    lane = lanes_of(shape)
    position = lax.rem(lane, GROUP)
    base = lane - position
    granted = layer < count
    one = jnp.where(granted, 1, 0)
    rank = one
    for step in (1, 2, 4):
        rank = rank + jnp.where(position >= step, pltpu.roll(rank, step, 1), 0)
    rank = rank - one
    number = group_total(one)
    offset = group_total(jnp.minimum(count, layer))
    target = lax.rem(offset + rank, GROUP)
    unpack_lane = base + target
    turn = lax.rem(position - offset + LAYERS * GROUP, GROUP)
    unpack_row = jnp.minimum((offset + turn) // GROUP, PACK_ROWS - 1)
    marked = jnp.where(granted, target, GROUP)
    pack_lane = lane
    for step in range(GROUP):
        if step == 0:
            seen = marked
        else:
            seen = jnp.where(
                position + step < GROUP, pltpu.roll(marked, W - step, 1), pltpu.roll(marked, GROUP - step, 1)
            )
        source = base + lax.rem(position + step, GROUP)
        pack_lane = jnp.where(seen == position, source, pack_lane)
    row = lax.broadcasted_iota(jnp.int32, (8, W), 0)
    pack_layer = jnp.zeros((8, W), jnp.int32)
    for r in range(PACK_ROWS):
        passed = jnp.where(offset + number <= GROUP * r + position, 1, 0)
        level = jnp.minimum(jnp.sum(passed, axis=0, keepdims=True), LAYERS - 1)
        pack_layer = jnp.where(row == r, level, pack_layer)
    return granted, pack_lane, pack_layer, unpack_row, unpack_lane


def along(x, index, axis):
    return jnp.take_along_axis(x, index, axis=axis, mode="promise_in_bounds")


def pack(x, tables):
    pack_lane, pack_layer = tables[1], tables[2]
    turned = [along(x[8 * i : 8 * i + 8], pack_lane[8 * i : 8 * i + 8], 1) for i in range(2)]
    within = lax.rem(pack_layer, 8)
    return jnp.where(pack_layer < 8, along(turned[0], within, 0), along(turned[1], within, 0))


def unpack(x, tables, first=0):
    granted, unpack_row, unpack_lane = tables[0], tables[3] + first, tables[4]
    parts = []
    for i in range(2):
        rows = slice(8 * i, 8 * i + 8)
        parts.append(along(along(x, unpack_row[rows], 0), unpack_lane[rows], 1))
    return jnp.where(granted, jnp.concatenate(parts, axis=0), 0.0)


def packed_start(i):
    return min(PACK_ROWS * i, 4 * PACK_ROWS - 8)


def slot_kernel(
    cells, ch_any, sym_any, lay_any, uid_any, power_any, neigh_any, coup_any, dft_any, twist_any, out,
    ch, sym, lay, uid, power, neigh, coup, dft, twist,
    sb, rb, hb, amp, lay_all, wsf, wrf, tx_own, tx_all, sig_all, sig_in, eas, ecol, scol, vs, wsb, w_out,
    symf, tmp, sy, wn, gf, lhs,
    ins, hs, hr, ts, tr, ss, sr, ws, wr, ready,
):
    ea, eb = eas.at[0], eas.at[1]
    fetches = [
        pltpu.make_async_copy(source, held, ins.at[i])
        for i, (source, held) in enumerate((
            (lay_any, lay), (uid_any, uid), (power_any, power), (ch_any, ch), (neigh_any, neigh),
            (coup_any, coup), (sym_any, sym), (dft_any, dft), (twist_any, twist),
        ))
    ]
    for fetch in fetches:
        fetch.start()
    me = lax.axis_index("lane")
    mc = lax.axis_index("cell")
    barrier = pltpu.get_barrier_semaphore()

    def lane_peer(d):
        return lax.rem(me + d, LANES)

    def cell_peer(d):
        return lax.rem(mc + d, cells)

    hub = me == 0

    def greet_lane(d, carry):
        peer = lane_peer(d)

        @pl.when(peer != 0)
        def _():
            pl.semaphore_signal(barrier, inc=1, device_id={"lane": peer}, device_id_type=MESH)

        return carry

    def greet_cell(d, _):
        pl.semaphore_signal(barrier, inc=1, device_id={"cell": cell_peer(d)}, device_id_type=MESH)
        return _

    lax.fori_loop(1, LANES, greet_lane, 0)
    @pl.when(hub)
    def _():
        lax.fori_loop(1, cells, greet_cell, 0)


    for fetch in fetches[:3]:
        fetch.wait()
    root = jnp.broadcast_to(jnp.sqrt(power[...]), (LAYERS, W))
    layer = lax.broadcasted_iota(jnp.int32, (LAYERS, W), 0)
    for h in range(2):
        part = slice(h * W, (h + 1) * W)
        picked = jnp.take_along_axis(root, uid[:, part], axis=1, mode="promise_in_bounds")
        granted = layer < lay[:, part]
        spread = swap4([lay[:, part]] * 4)
        for q in range(4):
            lay_all[4 * h + q] = spread[q]
        amplitude = jnp.where(granted, picked, 0.0)
        tx_own[h : h + 1, :] = jnp.sum(amplitude * amplitude, axis=0, keepdims=True) / LAYERS
        spread = swap4([amplitude] * 4)
        for q in range(4):
            amp[4 * h + q] = spread[q]

    def tx_copy(d):
        return pltpu.make_async_remote_copy(
            src_ref=tx_own, dst_ref=tx_all.at[mc], send_sem=ts, recv_sem=tr,
            device_id={"cell": cell_peer(d)}, device_id_type=MESH,
        )

    @pl.when(hub)
    def _():
        pl.semaphore_wait(barrier, cells - 1)
        for d in range(1, cells):
            tx_copy(d).start()

    natural = [pack_tables(lay[:, h * W : (h + 1) * W]) for h in range(2)]
    fetches[3].wait()
    for h in range(2):
        part = slice(h * W, (h + 1) * W)
        for ah in range(2):
            for c in range(2):
                turned = swap4([pack(ch[ah * 4 + g, c, :, part], natural[h]) for g in range(4)])
                first = PACK_ROWS * (2 * ah + c)
                for q in range(4):
                    sb[4 * h + q, first : first + PACK_ROWS, :] = turned[q][:PACK_ROWS]
    own_amp = amp[me]

    def block_copy(src, dst, send, recv, d):
        return pltpu.make_async_remote_copy(
            src_ref=src.at[lane_peer(d)], dst_ref=dst.at[me],
            send_sem=send.at[d - 1], recv_sem=recv.at[d - 1],
            device_id={"lane": lane_peer(d)}, device_id_type=MESH,
        )

    def sigma_copy(z):
        return pltpu.make_async_remote_copy(
            src_ref=sig_all.at[z], dst_ref=sig_in, send_sem=ss.at[z - 1], recv_sem=sr,
            device_id={"lane": z}, device_id_type=MESH,
        )

    far_first = (4, 3, 5, 2, 6, 1, 7)
    @pl.when(hub)
    def _():
        pl.semaphore_wait(ready, LANES - 1)

    @pl.when(me != 0)
    def _():
        pl.semaphore_wait(barrier, LANES - 1)

        pl.semaphore_signal(ready, inc=1, device_id={"lane": 0}, device_id_type=MESH)

    for d in far_first:
        block_copy(sb, rb, hs, hr, d).start()

    @pl.when(hub)
    def _():
        tx_all[mc] = tx_own[...]
        fetches[4].wait()
        fetches[5].wait()

        arrived = tx_all.at[pl.ds(0, cells - 1)]
        pltpu.make_async_copy(arrived, arrived, tr).wait()
        sigma = jnp.full((2, W), NOISE_FLOOR, F32)
        for k in range(neigh.shape[0]):
            sigma = sigma + coup[k, mc] * tx_all[neigh[k, mc]]
        for h in range(2):
            spread = swap4([sigma[h : h + 1, :]] * 4)
            for q in range(4):
                sig_all[4 * h + q] = spread[q]
        for z in far_first:
            sigma_copy(z).start()
        sig_in[...] = sig_all[0]

    @pl.when(me != 0)
    def _():
        fetches[4].wait()
        fetches[5].wait()

    own_tables = pack_tables(lay_all[me])

    def unpack_block(source, z):
        for ah in range(2):
            for c in range(2):
                i = 2 * ah + c
                first = packed_start(i)
                hb[2 * z + ah, c] = unpack(
                    source[z, first : first + 8, :], own_tables, PACK_ROWS * i - first
                )
            hb[2 * z + ah, 2] = hb[2 * z + ah, 0] + hb[2 * z + ah, 1]

    unpack_block(sb, me)
    fetches[6].wait()
    spread_symbols(sym, symf, tmp, sy)

    def take_block(z):
        @pl.when(me != z)
        def _():
            block_copy(sb, rb, hs, hr, lax.rem(me - z + LANES, LANES)).wait_recv()
            unpack_block(rb, z)

    for z in range(1, LANES):
        take_block(z)

    zero = jnp.zeros((8, W), F32)
    for lt in range(2):
        rows = slice(8 * lt, 8 * lt + 8)

        def gram_step(a, acc, rows=rows):
            ar, ai = hb[a, 0, rows, :], hb[a, 1, rows, :]
            out = []
            for m in range(LAYERS):
                br, bi = hb[a, 0, m : m + 1, :], hb[a, 1, m : m + 1, :]
                out.append(acc[2 * m] + (ar * br + ai * bi))
                out.append(acc[2 * m + 1] + (ai * br - ar * bi))
            return tuple(out)

        acc = lax.fori_loop(2, 2 * LANES, gram_step, (zero,) * (2 * LAYERS))
        for m in range(LAYERS):
            ea[0, m, rows, :] = acc[2 * m]
            ea[1, m, rows, :] = acc[2 * m + 1]

    take_block(0)
    for lt in range(2):
        rows = slice(8 * lt, 8 * lt + 8)
        for m in range(LAYERS):
            gr, gi = ea[0, m, rows, :], ea[1, m, rows, :]
            for a in range(2):
                ar, ai = hb[a, 0, rows, :], hb[a, 1, rows, :]
                br, bi = hb[a, 0, m : m + 1, :], hb[a, 1, m : m + 1, :]
                gr = gr + (ar * br + ai * bi)
                gi = gi + (ai * br - ar * bi)
            ea[0, m, rows, :] = total4(gr)
            ea[1, m, rows, :] = total4(gi)

    @pl.when(me != 0)
    def _():
        sigma_copy(1).wait_recv()

    @pl.when(hub)
    def _():
        for z in range(1, LANES):
            sigma_copy(z).wait_send()
        arrived = tx_all.at[pl.ds(0, cells - 1)]
        pltpu.make_async_copy(arrived, arrived, ts).wait()

    sigma = sig_in[...]
    diagonal = jnp.zeros((LAYERS, W), F32)
    for m in range(LAYERS):
        diagonal = diagonal + jnp.where(layer == m, ea[0, m] + sigma, 0.0)
    inv_trace = 1.0 / jnp.sum(diagonal, axis=0, keepdims=True)
    for m in range(LAYERS):
        ea[0, m] = jnp.where(layer == m, 1.0 - (ea[0, m] + sigma) * inv_trace, -ea[0, m] * inv_trace)
        ea[1, m] = -ea[1, m] * inv_trace
        ea[2, m] = ea[0, m] + ea[1, m]
    column = lanes_of((LAYERS, W)) // 32
    for j in range(4):
        for c in range(2):
            ecol[c, j] = pick4([ea[c, 4 * j + g] for g in range(4)])
        scol[0, j] = ecol[0, j] + jnp.where(layer == 4 * j + column, 1.0, 0.0)
        scol[1, j] = ecol[1, j]
        ecol[2, j] = ecol[0, j] + ecol[1, j]
        scol[2, j] = scol[0, j] + scol[1, j]

    def products(refs, held_in):
        sums = [[[jnp.zeros((LAYERS, W), F32) for j in range(4)] for c in range(3)] for _ in refs]
        for c in range(3):
            for k in range(LAYERS):
                left = held_in[c, k]
                for ref, held in zip(refs, sums):
                    for j in range(4):
                        held[c][j] = held[c][j] + left * ref[c, j, k : k + 1, :]
        return [
            (
                [held[0][j] - held[1][j] for j in range(4)],
                [held[2][j] - (held[0][j] + held[1][j]) for j in range(4)],
            )
            for held in sums
        ]

    def put_square(square, to):
        for c in range(2):
            for j in range(4):
                ecol[c, j] = square[c][j]
        for j in range(4):
            ecol[2, j] = square[0][j] + square[1][j]
        for j in range(4):
            real, imag = spread4(square[0][j]), spread4(square[1][j])
            for g in range(4):
                to[0, 4 * j + g] = real[g]
                to[1, 4 * j + g] = imag[g]
                to[2, 4 * j + g] = real[g] + imag[g]

    put_square(products([ecol], ea)[0], eb)

    def level(i, _):
        for held_in, to in ((eb, ea), (ea, eb)):
            put_square(products([ecol], held_in)[0], to)
            (more,) = products([scol], held_in)
            for j in range(4):
                for c in range(2):
                    scol[c, j] = scol[c, j] + more[c][j]
                scol[2, j] = scol[0, j] + scol[1, j]
        return _

    lax.fori_loop(0, 2, level, 0)
    (more,) = products([scol], eb)
    for j in range(4):
        last = [(scol[c, j] + more[c][j]) * inv_trace for c in range(2)]
        real, imag = spread4(last[0]), spread4(last[1])
        for g in range(4):
            ea[0, 4 * j + g] = real[g]
            ea[1, 4 * j + g] = imag[g]
            ea[2, 4 * j + g] = real[g] + imag[g]

    def apply_step(z, energy):
        sums = [[jnp.zeros((LAYERS, W), F32) for c in range(3)] for a in range(4)]
        for c in range(3):
            for m in range(LAYERS):
                right = ea[c, m]
                for a in range(4):
                    sums[a][c] = sums[a][c] + hb[4 * z + a, c, m : m + 1, :] * right
        for a in range(4):
            vr = sums[a][0] - sums[a][1]
            vi = (sums[a][0] + sums[a][1]) - sums[a][2]
            vs[4 * z + a, 0] = vr
            vs[4 * z + a, 1] = vi
            energy = energy + (vr * vr + vi * vi)
        return energy

    energy = total4(lax.fori_loop(0, LANES // 2, apply_step, jnp.zeros((LAYERS, W), F32)))
    scale = own_amp / jnp.sqrt(energy + NORM_EPS)

    def round_block(z, target):
        for ah in range(2):
            for c in range(2):
                first = PACK_ROWS * (2 * ah + c)
                wsf[z, first : first + PACK_ROWS, :] = pack(vs[2 * z + ah, c] * scale, own_tables)[:PACK_ROWS]
        target[z] = wsf[z].astype(BF16)

    for d in far_first:
        round_block(lane_peer(d), wsb)
        block_copy(wsb, w_out, ws, wr, d).start()
    round_block(me, w_out)
    natural = [pack_tables(lay[:, h * W : (h + 1) * W]) for h in range(2)]
    for d in far_first[::-1]:
        block_copy(wsb, w_out, ws, wr, d).wait()
    for d in far_first:
        block_copy(sb, rb, hs, hr, d).wait_send()
    for z in range(LANES):
        wrf[z] = w_out[z].astype(F32)

    for h in range(2):
        for ah in range(2):
            for c in range(2):
                i = 2 * ah + c
                first = packed_start(i)
                turned = swap4([wrf[4 * h + q, first : first + 8, :] for q in range(4)])
                for g in range(4):
                    wn[h, ah * 4 + g, c] = unpack(turned[g], natural[h], PACK_ROWS * i - first)
            for g in range(4):
                wn[h, ah * 4 + g, 2] = wn[h, ah * 4 + g, 0] + wn[h, ah * 4 + g, 1]

    for h in range(2):

        def precode(half, _, h=h):
            sums = [[[jnp.zeros((8, W), F32) for i in range(3)] for c in range(3)] for a in range(4)]
            for l in range(LAYERS):
                for c in range(3):
                    first = (c * LAYERS + l) * 24
                    right = [sy[h, first + 8 * i : first + 8 * i + 8, :] for i in range(3)]
                    for a in range(4):
                        left = wn[h, 4 * half + a, c, l : l + 1, :]
                        for i in range(3):
                            sums[a][c][i] = sums[a][c][i] + left * right[i]
            for a in range(4):
                for i in range(3):
                    p0, p1, p2 = sums[a][0][i], sums[a][1][i], sums[a][2][i]
                    sums[a][0][i] = p0 - p1
                    sums[a][1][i] = p2 - (p0 + p1)
            for a in range(4):
                for c in range(2):
                    for i in range(3):
                        gf[c, h, pl.ds(64 * i + 4 * half + a, 8, stride=8), :] = sums[a][c][i]
            return _

        lax.fori_loop(0, 2, precode, 0)

    for c in range(2):
        for h in range(2):
            value = gf[c, h]
            high = value.astype(BF16)
            cols = slice(c * PRBS + h * W, c * PRBS + (h + 1) * W)
            lhs[:, cols] = high

    fetches[7].wait()
    fetches[8].wait()

    def section(nt):
        result = jnp.dot(lhs[...], dft[nt], preferred_element_type=F32)
        for s in range(SYMS):
            part = [[None, None] for _ in range(4)]
            for k in range(SUBC):
                row = (s * SUBC + k) * 8
                tr, ti = result[row : row + 8, 0:W], result[row : row + 8, W : 2 * W]
                cr, ci = twist[nt, k : k + 1, :], twist[nt, SUBC + k : SUBC + k + 1, :]
                ur, ui = tr * cr - ti * ci, tr * ci + ti * cr
                held = part[k % 4]
                held[0] = ur if held[0] is None else held[0] + ur
                held[1] = ui if held[1] is None else held[1] + ui
            (ar, ai), (br, bi), (cr, ci), (dr, di) = part
            pr, pi, mr, mi = ar + cr, ai + ci, ar - cr, ai - ci
            qr, qi, nr, ni = br + dr, bi + di, br - dr, bi - di
            outs = ((pr + qr, pi + qi), (mr - ni, mi + nr), (pr - qr, pi - qi), (mr + ni, mi - nr))
            for n2 in range(4):
                for c in range(2):
                    out[pl.ds(c * 64 + (n2 * 8 + nt) * 2 + s, 8, stride=128), :] = outs[n2][c]

    def sections(i, _):
        for step in range(4):
            section(4 * i + step)
        return _

    lax.fori_loop(0, 2, sections, 0)


def ofdm_tables():
    p = np.arange(PRBS)[:, None]
    n = np.arange(1024)[None, :]
    angle = 2.0 * math.pi * ((3 * p * n) % 1024) / 1024
    cos, sin = np.cos(angle), np.sin(angle)
    real = np.concatenate([cos, -sin], 0).reshape(2 * PRBS, 8, 1, W)
    imag = np.concatenate([sin, cos], 0).reshape(2 * PRBS, 8, 1, W)
    dft = np.concatenate([real, imag], 2).reshape(2 * PRBS, 8, 2 * W).transpose(1, 0, 2)
    k = np.arange(SUBC)[:, None]
    angle = 2.0 * math.pi * (((k - 1536) * n) % NFFT) / NFFT
    twist = np.concatenate([np.cos(angle), np.sin(angle)], 0) / math.sqrt(NFFT)
    twist = twist.reshape(2 * SUBC, 8, W).transpose(1, 0, 2)
    return jnp.asarray(dft, BF16), jnp.asarray(twist, F32)


def slot(cells, channel, symbols, layers, user_ids, user_power, neighbours, coupling):
    dft, twist = ofdm_tables()
    args = (channel, symbols, layers, user_ids, user_power, neighbours, coupling, dft, twist)
    block = (2 * LANES, 2, LAYERS, W)
    packed = (LANES, 4 * PACK_ROWS, W)
    dma = pltpu.SemaphoreType.DMA
    held = [(pltpu.SMEM if i in (5, 6) else pltpu.VMEM)(x.shape, x.dtype) for i, x in enumerate(args)]
    return pl.pallas_call(
        functools.partial(slot_kernel, cells),
        out_shape=pltpu.VMEM((1024, W), F32),
        in_specs=[pl.BlockSpec(memory_space=pl.ANY)] * len(args),
        out_specs=pl.BlockSpec(memory_space=pltpu.VMEM),
        scratch_shapes=held + [
            pltpu.VMEM(packed, F32),
            pltpu.VMEM(packed, F32),
            pltpu.VMEM((2 * LANES, 3, LAYERS, W), F32),
            pltpu.VMEM((LANES, LAYERS, W), F32),
            pltpu.VMEM((LANES, 1, W), jnp.int32),
            pltpu.VMEM(packed, F32),
            pltpu.VMEM(packed, F32),
            pltpu.VMEM((2, W), F32),
            pltpu.VMEM((cells, 2, W), F32),
            pltpu.VMEM((LANES, 1, W), F32),
            pltpu.VMEM((1, W), F32),
            pltpu.VMEM((2, 3, LAYERS, LAYERS, W), F32),
            pltpu.VMEM((3, 4, LAYERS, W), F32),
            pltpu.VMEM((3, 4, LAYERS, W), F32),
            pltpu.VMEM(block, F32),
            pltpu.VMEM(packed, BF16),
            pltpu.VMEM(packed, BF16),
            pltpu.VMEM((64, 3072), F32),
            pltpu.VMEM((8, 64, 384), F32),
            pltpu.VMEM((2, 1152, W), F32),
            pltpu.VMEM((2, 8, 3, LAYERS, W), F32),
            pltpu.VMEM((2, 2, 192, W), F32),
            pltpu.VMEM((192, 512), BF16),
            dma((len(args),)),
            dma((LANES - 1,)),
            dma((LANES - 1,)),
            dma,
            dma,
            dma((LANES - 1,)),
            dma,
            dma((LANES - 1,)),
            dma((LANES - 1,)),
            pltpu.SemaphoreType.REGULAR,
        ],
        compiler_params=pltpu.CompilerParams(collective_id=0, has_side_effects=True),
        name="slot",
    )(*args)


def per_device(cells, channel, symbols, layers, user_ids, user_power, neighbours, coupling):
    samples = slot(
        cells, channel[0], symbols[0].reshape(2 * LAYERS, SYMS, 3072), layers, user_ids[0], user_power,
        neighbours.T, coupling.T,
    )
    samples = samples.reshape(8, 2, 32, SYMS, W).transpose(0, 1, 3, 2, 4)
    return samples.reshape(1, 8, 2, SYMS, NFFT)


def solution(mesh):
    in_specs = (
        P("cell", "lane", None, None, None),
        P("cell", None, None, None, None),
        P("cell", None),
        P("cell", None, None),
        P("cell", None),
        P(),
        P(),
    )
    out_specs = P("cell", "lane", None, None, None)
    return jax.shard_map(
        functools.partial(per_device, mesh.shape["cell"]),
        mesh=mesh, in_specs=in_specs, out_specs=out_specs, check_vma=False,
    )
```
